32 devices in a mesh: parts: 2 (over y), seq: 4 (over z), sub: 4 (over x, core).
Axes of the slice: x: 2, y: 2, z: 4, core: 2. Of those that a mesh axis runs over, the one named last changes fastest.
Arguments:
- q_space: bfloat16 [16, 512, 2048], P(('parts', 'seq'), None, 'sub'), parts along dimension 0, may hold values from -6 to 6
- k_space: bfloat16 [16, 512, 2048], P(('parts', 'seq'), None, 'sub'), parts along dimension 0, may hold values from -6 to 6
- v_space: bfloat16 [16, 512, 2048], P(('parts', 'seq'), None, 'sub'), parts along dimension 0, may hold values from -6 to 6
- q_time: bfloat16 [16, 4, 128, 2048], P('parts', None, 'seq', 'sub'), parts along dimension 0, may hold values from -6 to 6
- k_time: bfloat16 [16, 4, 128, 2048], P('parts', None, 'seq', 'sub'), parts along dimension 0, may hold values from -6 to 6
- out_weight: bfloat16 [2048, 3072], P('sub', 'seq'), may hold values from -0.125 to 0.125
- cotangent: bfloat16 [16, 512, 3072], P(('parts', 'seq'), 'sub'), parts along dimension 0, may hold values from -6 to 6
Outputs:
- dq_space: bfloat16 [16, 512, 2048], P(('parts', 'seq'), None, 'sub'), parts along dimension 0
- dk_space: bfloat16 [16, 512, 2048], P(('parts', 'seq'), None, 'sub'), parts along dimension 0
- dv_space: bfloat16 [16, 512, 2048], P(('parts', 'seq'), None, 'sub'), parts along dimension 0
- d_weight: float32 [4096, 3072], P(('parts', 'sub'), 'seq'), parts along dimension 0
The draws below stay inside these ranges and needn't reach their ends.
There are 2 independent parts, one for each index of `parts`. The reference program is written for one: setup_inputs(seed, part) draws one part's arguments, and reference() takes and returns one part's arrays. A program takes and returns all parts, laid end to end along the dimension named above; an argument that names none is the same for every part. Nothing has to cross between parts.
All inputs are finite; a program needn't handle non-finite values.
Results may differ from the reference program's by a relative error of at most 0.01.
Values may be sent and summed in bfloat16 or wider, within the bound.
No kernel may reach another device: no remote copies, remote signals or barrier semaphores. Data moves between devices by JAX's collectives and lax.ppermute only.
A program may use at most 128 MiB of HBM per device.

```python
import math
import jax
import jax.numpy as jnp
from jax import lax

D = 3072
HEADS = 16
HD = 128
P_SIZE = 512
HH = 2048
F = 8
BANDS = 4
PSUB = 128


def noisy(key, salt, shape):
    values = jnp.clip(jax.random.normal(jax.random.fold_in(key, salt), shape, jnp.float32), -5.0, 5.0)
    return values


def draw_q_space(key, part):
    values = noisy(key, 11, (F, P_SIZE, HH))
    return values.astype(jnp.bfloat16)


def draw_k_space(key, part):
    values = noisy(key, 21, (F, P_SIZE, HH))
    return values.astype(jnp.bfloat16)


def draw_q_time(key, part):
    values = noisy(key, 31, (F, BANDS, PSUB, HH))
    return values.astype(jnp.bfloat16)


def draw_k_time(key, part):
    values = noisy(key, 41, (F, BANDS, PSUB, HH))
    return values.astype(jnp.bfloat16)


def spiked(array, key, source, target, parts, factor):
    def block_of(dim):
        return (jnp.arange(array.shape[dim]) // (array.shape[dim] // parts)).reshape((-1,) + (1,) * (array.ndim - 1 - dim))

    first = jax.random.permutation(key, parts)[block_of(target)]
    far = (block_of(target) + parts // 2) % parts
    return jnp.where((block_of(source) == first) | (block_of(source) == far), factor * array, array)


def shard_levels(stream_key, dims, shards, smallest, largest):
    level, own = 1.0, jax.random.fold_in(stream_key, 6)
    for dim, parts in shards:
        steps = jnp.exp(jax.random.uniform(jax.random.fold_in(own, dim), (parts,), jnp.float32, smallest / len(shards), largest / len(shards)))
        level = level * jnp.repeat(steps, dims[dim] // parts).reshape([-1 if axis == dim else 1 for axis in range(len(dims))])
    return level


def centred(own_key, shape, scale, limit, shards=(), dtype=jnp.bfloat16):
    entries = scale * jax.random.normal(own_key, shape, jnp.float32)
    if shards:
        entries = entries * shard_levels(own_key, shape, shards, -0.22, 0.18)
    return jnp.clip(entries, -limit, limit).astype(dtype)


def bell_draw_with(stream_key, extent, scale, limit, cuts, heavy, dtype=jnp.bfloat16):
    result = scale * jax.random.normal(stream_key, extent, jnp.float32)
    if cuts:
        result = result * shard_levels(stream_key, extent, cuts, -0.22, 0.18)
    return jnp.clip(spiked(result, jax.random.fold_in(stream_key, 3), *heavy), -limit, limit).astype(dtype)


def setup_inputs(seed: int = 0, part: int = 0) -> dict:
    seeds = jax.random.split(jax.random.key(seed), 8)
    own_keys = jax.random.split(jax.random.fold_in(seeds[7], part), 8)
    q_space = draw_q_space(jax.random.fold_in(jax.random.fold_in(seeds[7], part), 71), part)
    k_space = draw_k_space(jax.random.fold_in(jax.random.fold_in(seeds[7], part), 71), part)
    v_space = centred(own_keys[2], (F, P_SIZE, HH), 1.0, 6.0, ((0, 4), (2, 4)))
    q_time = draw_q_time(jax.random.fold_in(jax.random.fold_in(seeds[7], part), 71), part)
    k_time = draw_k_time(jax.random.fold_in(jax.random.fold_in(seeds[7], part), 71), part)
    out_weight = centred(seeds[5], (HH, D), HH ** -0.5, 0.125, ((0, 4), (1, 4)))
    cotangent = bell_draw_with(own_keys[6], (F, P_SIZE, D), 1.0, 6.0, ((0, 4), (1, 4)), (0, 2, 4, 2.0))
    return dict(q_space=q_space, k_space=k_space, v_space=v_space, q_time=q_time, k_time=k_time, out_weight=out_weight, cotangent=cotangent)


def normalize(scores):
    row_top = lax.optimization_barrier(jnp.max(scores, axis=-1, keepdims=True))
    raised = jnp.exp(scores - row_top)
    return raised / lax.optimization_barrier(jnp.sum(raised, axis=-1, keepdims=True))

def rounded_back(values):
    return lax.optimization_barrier(values.astype(jnp.bfloat16)).astype(jnp.float32)

def space_forward(inputs):
    query, keys, values = inputs
    scores = jnp.einsum('qhd,khd->hqk', query.astype(jnp.float32), keys.astype(jnp.float32)) * (1.0 / math.sqrt(HD))
    chances = rounded_back(normalize(scores))
    return jnp.einsum('hqk,khd->qhd', chances, values.astype(jnp.float32)).astype(jnp.bfloat16)

def space_backward(inputs):
    query, keys, values, upstream = inputs
    query_f = query.astype(jnp.float32)
    keys_f = keys.astype(jnp.float32)
    upstream_f = upstream.astype(jnp.float32)
    scores = jnp.einsum('qhd,khd->hqk', query_f, keys_f) * (1.0 / math.sqrt(HD))
    chances = normalize(scores)
    value_grad = jnp.einsum('hqk,qhd->khd', rounded_back(chances), upstream_f).astype(jnp.bfloat16)
    chance_grad = jnp.einsum('qhd,khd->hqk', upstream_f, values.astype(jnp.float32))
    centre_term = lax.optimization_barrier(jnp.sum(chances * chance_grad, axis=-1, keepdims=True))
    score_grad = rounded_back(chances * (chance_grad - centre_term) * (1.0 / math.sqrt(HD)))
    query_grad = jnp.einsum('hqk,khd->qhd', score_grad, keys_f).astype(jnp.bfloat16)
    keys_grad = jnp.einsum('hqk,qhd->khd', score_grad, query_f).astype(jnp.bfloat16)
    return (query_grad, keys_grad, value_grad)

def reference(q_space, k_space, v_space, q_time, k_time, out_weight, cotangent):
    split_shape = (F, P_SIZE, HEADS, HD)
    space_query = q_space.reshape(split_shape)
    space_keys = k_space.reshape(split_shape)
    space_values = v_space.reshape(split_shape)
    space_out = lax.map(space_forward, (space_query, space_keys, space_values))
    time_query = q_time.reshape(split_shape).astype(jnp.float32)
    time_keys = k_time.reshape(split_shape).astype(jnp.float32)
    time_scores = jnp.einsum('fphd,gphd->phfg', time_query, time_keys) * (1.0 / math.sqrt(HD))
    time_chances = rounded_back(normalize(time_scores))
    time_out = jnp.einsum('phfg,gphd->fphd', time_chances, space_out.astype(jnp.float32)).astype(jnp.bfloat16)
    flat_cot = cotangent.reshape(F * P_SIZE, D)
    time_grad = jnp.dot(flat_cot, out_weight.T, preferred_element_type=jnp.float32).astype(jnp.bfloat16)
    d_weight = jnp.dot(time_out.reshape(F * P_SIZE, HH).T, flat_cot, preferred_element_type=jnp.float32)
    space_grad = jnp.einsum('phfg,fphd->gphd', time_chances, time_grad.reshape(split_shape).astype(jnp.float32)).astype(jnp.bfloat16)
    query_grad, keys_grad, value_grad = lax.map(space_backward, (space_query, space_keys, space_values, space_grad))
    return (query_grad.reshape(F, P_SIZE, HH), keys_grad.reshape(F, P_SIZE, HH), value_grad.reshape(F, P_SIZE, HH), d_weight)
```

```python
import functools
import math

import jax
import jax.numpy as jnp
from jax import lax
from jax.experimental import pallas as pl
from jax.experimental.pallas import tpu as pltpu
from jax.sharding import PartitionSpec as P

HD = 128
SCALE = 1.0 / math.sqrt(HD)


def normalize(scores):
    row_top = jnp.max(scores, axis=-1, keepdims=True)
    raised = jnp.exp(scores - row_top)
    return raised / jnp.sum(raised, axis=-1, keepdims=True)


def space_chances(query, keys):
    scores = jnp.einsum("fqhd,fkhd->fhqk", query, keys, preferred_element_type=jnp.float32) * (
        1.0 / math.sqrt(HD)
    )
    return normalize(scores)


def on_device(q_space, k_space, v_space, q_time, k_time, out_weight, cotangent):
    frame_count, patches, columns = q_space.shape
    head_count = columns // HD
    band_count = lax.axis_size("sub")
    seq_count = lax.axis_size("seq")
    all_frames = frame_count * seq_count
    band_len = patches // band_count
    time_len = band_len // seq_count
    split_shape = (frame_count, patches, head_count, HD)
    space_query = q_space.reshape(split_shape)
    space_keys = k_space.reshape(split_shape)
    space_values = v_space.reshape(split_shape)
    chances = space_chances(space_query, space_keys)
    space_out = jnp.einsum(
        "fhqk,fkhd->fqhd",
        chances.astype(jnp.bfloat16),
        space_values,
        preferred_element_type=jnp.float32,
    ).astype(jnp.bfloat16)
    moved = lax.all_to_all(
        space_out.reshape(frame_count, band_count, band_len, columns),
        "seq",
        split_axis=2,
        concat_axis=0,
        tiled=True,
    )
    time_shape = (all_frames, band_count, time_len, head_count, HD)
    time_query = q_time.reshape(time_shape)
    time_keys = k_time.reshape(time_shape)
    time_values = moved.reshape(time_shape)
    time_scores = jnp.einsum(
        "fbphd,gbphd->bphfg", time_query, time_keys, preferred_element_type=jnp.float32
    ) * (1.0 / math.sqrt(HD))
    time_chances = normalize(time_scores).astype(jnp.bfloat16)
    time_out = jnp.einsum(
        "bphfg,gbphd->fbphd", time_chances, time_values, preferred_element_type=jnp.float32
    ).astype(jnp.bfloat16)
    time_out = time_out.reshape(all_frames, band_count, time_len, columns)
    weight_rows = lax.all_gather(out_weight, "seq", axis=1, tiled=True)
    returned = lax.all_to_all(time_out, "seq", split_axis=0, concat_axis=2, tiled=True)
    frame_out = returned.reshape(frame_count, patches, columns)
    segment = lax.all_gather(cotangent, "sub", axis=1, tiled=True)
    weight_sum = jnp.einsum("fnh,fnd->hd", frame_out, segment, preferred_element_type=jnp.float32)
    update = jnp.einsum("fnd,hd->fnh", segment, weight_rows, preferred_element_type=jnp.float32)
    out_grad = update
    weight_sum, out_grad = (weight_sum, out_grad)
    rounded = out_grad.astype(jnp.bfloat16).reshape(frame_count, band_count, band_len, columns)
    time_grad = lax.all_to_all(rounded, "seq", split_axis=2, concat_axis=0, tiled=True)
    d_weight = lax.psum_scatter(
        weight_sum.astype(jnp.bfloat16), "seq", scatter_dimension=1, tiled=True
    ).astype(jnp.float32)
    value_time = jnp.einsum(
        "bphfg,fbphd->gbphd",
        time_chances,
        time_grad.reshape(time_shape),
        preferred_element_type=jnp.float32,
    ).astype(jnp.bfloat16)
    space_grad = lax.all_to_all(
        value_time.reshape(all_frames, band_count, time_len, columns),
        "seq",
        split_axis=0,
        concat_axis=2,
        tiled=True,
    )
    space_grad = space_grad.reshape(split_shape)
    recomputed = space_chances(space_query, space_keys)
    value_grad = jnp.einsum(
        "fhqk,fqhd->fkhd",
        recomputed.astype(jnp.bfloat16),
        space_grad,
        preferred_element_type=jnp.float32,
    ).astype(jnp.bfloat16)
    chance_grad = jnp.einsum(
        "fqhd,fkhd->fhqk", space_grad, space_values, preferred_element_type=jnp.float32
    )
    centre_term = jnp.sum(recomputed * chance_grad, axis=-1, keepdims=True)
    score_grad = (recomputed * (chance_grad - centre_term) * (1.0 / math.sqrt(HD))).astype(
        jnp.bfloat16
    )
    query_grad = jnp.einsum(
        "fhqk,fkhd->fqhd", score_grad, space_keys, preferred_element_type=jnp.float32
    ).astype(jnp.bfloat16)
    keys_grad = jnp.einsum(
        "fhqk,fqhd->fkhd", score_grad, space_query, preferred_element_type=jnp.float32
    ).astype(jnp.bfloat16)
    flat_shape = (frame_count, patches, columns)
    return (
        query_grad.reshape(flat_shape),
        keys_grad.reshape(flat_shape),
        value_grad.reshape(flat_shape),
        d_weight,
    )


def xor_send(value, axis, distance):
    count = lax.axis_size(axis)
    return lax.ppermute(value, axis, [(i, i ^ distance) for i in range(count)])


def swap_parts(value):
    return lax.ppermute(value, "parts", [(0, 1), (1, 0)])


def nt_dot(a, b):
    return lax.dot_general(a, b, (((1,), (1,)), ((), ())), preferred_element_type=jnp.float32)


def tn_dot(a, b):
    return lax.dot_general(a, b, (((0,), (0,)), ((), ())), preferred_element_type=jnp.float32)


def nn_dot(a, b):
    return lax.dot_general(a, b, (((1,), (0,)), ((), ())), preferred_element_type=jnp.float32)


def softmax_rows(scores, scale, axis):
    raised = jnp.exp((scores - jnp.max(scores, axis=axis, keepdims=True)) * scale)
    return raised * (1.0 / jnp.sum(raised, axis=axis, keepdims=True))


def params():
    return pltpu.CompilerParams(vmem_limit_bytes=56 * 1024 * 1024)


def space_forward_kernel(ids, q, k, v, *rest):
    seq_count, (probs, spare) = len(rest) - 2, rest[-2:]
    me = ids[0]
    low = softmax_rows(nt_dot(k[0], q[0]), SCALE, 0).astype(jnp.bfloat16)
    probs[0] = low
    out = tn_dot(v[0], low).T.astype(jnp.bfloat16)
    spare[...] = out.reshape(spare.shape)
    for step in range(seq_count):
        rest[step][0] = spare[:, me ^ step]


def space_forward(ids, q, k, v, seq_count, band_count, time_len):
    frames, patches, columns = q.shape
    heads = columns // HD
    wide = pl.BlockSpec((1, patches, HD), lambda f, h, ids: (f, 0, h))
    piece = pl.BlockSpec((1, band_count, time_len, HD), lambda f, h, ids: (f, 0, 0, h))
    piece_shape = jax.ShapeDtypeStruct((frames, band_count, time_len, columns), jnp.bfloat16)
    square = pl.BlockSpec((1, patches, patches), lambda f, h, ids: (f * heads + h, 0, 0))
    square_shape = jax.ShapeDtypeStruct((frames * heads, patches, patches), jnp.bfloat16)
    outs = pl.pallas_call(
        space_forward_kernel,
        grid_spec=pltpu.PrefetchScalarGridSpec(
            num_scalar_prefetch=1,
            grid=(frames, heads),
            in_specs=[wide, wide, wide],
            out_specs=[piece] * seq_count + [square],
            scratch_shapes=[pltpu.VMEM((band_count, seq_count, time_len, HD), jnp.bfloat16)],
        ),
        out_shape=[piece_shape] * seq_count + [square_shape],
        compiler_params=params(),
        name="space_forward",
    )(ids, q, k, v)
    return outs[:seq_count], outs[seq_count]


def time_probs_kernel(ids, q, k, probs, probs_t, *, seq_count):
    me = ids[0]
    frames, _, time_len, _ = q.shape
    local = frames // seq_count
    rows = frames * time_len

    def ordered(ref):
        picked = [ref[pl.ds((me ^ step) * local, local), 0] for step in range(seq_count)]
        return jnp.concatenate(picked, axis=0).reshape(rows, HD)

    query, keys = ordered(q), ordered(k)
    place = [lax.broadcasted_iota(jnp.int32, (rows, rows), axis) % time_len for axis in (0, 1)]
    same = place[0] == place[1]
    low = jnp.float32(-1e30)
    probs[0, 0] = softmax_rows(jnp.where(same, nt_dot(query, keys), low), SCALE, 1).astype(jnp.bfloat16)
    probs_t[0, 0] = softmax_rows(jnp.where(same, nt_dot(keys, query), low), SCALE, 0).astype(jnp.bfloat16)


def time_probs(ids, q, k, seq_count):
    frames, bands, time_len, columns = q.shape
    heads = columns // HD
    rows = frames * time_len
    spec = pl.BlockSpec((frames, 1, time_len, HD), lambda r, h, ids: (0, ids[1] ^ r, 0, h))
    square = pl.BlockSpec((1, 1, rows, rows), lambda r, h, ids: (r, h, 0, 0))
    square_shape = jax.ShapeDtypeStruct((bands, heads, rows, rows), jnp.bfloat16)
    return pl.pallas_call(
        functools.partial(time_probs_kernel, seq_count=seq_count),
        grid_spec=pltpu.PrefetchScalarGridSpec(
            num_scalar_prefetch=1,
            grid=(bands, heads),
            in_specs=[spec, spec],
            out_specs=[square, square],
        ),
        out_shape=[square_shape, square_shape],
        compiler_params=params(),
        name="time_probs",
    )(ids, q, k)


def time_out_kernel(ids, probs, *rest):
    out = rest[-1]
    rows = probs.shape[2]
    for head in range(probs.shape[1]):
        lanes = slice(head * HD, (head + 1) * HD)
        values = jnp.concatenate([ref[:, 0, :, lanes] for ref in rest[:-1]], axis=0).reshape(rows, HD)
        out[0, :, lanes] = nn_dot(probs[0, head], values).astype(jnp.bfloat16)


def time_out(ids, probs, pieces):
    bands, heads, rows, _ = probs.shape
    local, _, time_len, columns = pieces[0].shape
    piece = pl.BlockSpec((local, 1, time_len, columns), lambda r, ids: (0, ids[1] ^ r, 0, 0))
    return pl.pallas_call(
        time_out_kernel,
        grid_spec=pltpu.PrefetchScalarGridSpec(
            num_scalar_prefetch=1,
            grid=(bands,),
            in_specs=[pl.BlockSpec((1, heads, rows, rows), lambda r, ids: (r, 0, 0, 0))] + [piece] * len(pieces),
            out_specs=pl.BlockSpec((1, rows, columns), lambda r, ids: (r, 0, 0)),
        ),
        out_shape=jax.ShapeDtypeStruct((bands, rows, columns), jnp.bfloat16),
        compiler_params=params(),
        name="time_out",
    )(ids, probs, *pieces)


def weight_grad_kernel(ids, left, *rest):
    out, width = rest[-1], rest[0].shape[-1]
    right = jnp.concatenate([ref[...].reshape(-1, width) for ref in rest[:-1]], axis=0)
    out[...] = tn_dot(left[...], right).astype(out.dtype)


def weight_grad(ids, left, cots, step, width, dtype):
    tokens, columns = left.shape
    tile = 256
    inner = width // tile
    local, time_len, _ = cots[0].shape
    cot_spec = pl.BlockSpec((local, time_len, tile), lambda j, ids: (0, 0, (ids[0] ^ step) * inner + j))
    return pl.pallas_call(
        weight_grad_kernel,
        grid_spec=pltpu.PrefetchScalarGridSpec(
            num_scalar_prefetch=1,
            grid=(inner,),
            in_specs=[pl.BlockSpec((tokens, columns), lambda j, ids: (0, 0))] + [cot_spec] * len(cots),
            out_specs=pl.BlockSpec((columns, tile), lambda j, ids: (0, j)),
        ),
        out_shape=jax.ShapeDtypeStruct((columns, width), dtype),
        compiler_params=params(),
        name="weight_grad",
    )(ids, left, *cots)


def space_grad_kernel(ids, probs_t, own, *rest, seq_count, band_count):
    mine, rest = rest[: seq_count - 1], rest[seq_count - 1 :]
    theirs, rest = rest[: seq_count - 1], rest[seq_count - 1 :]
    cots, outs, weight = rest[: band_count * seq_count], rest[-1 - seq_count : -1], rest[-1]
    me, sub, part = ids[0], ids[1], ids[2]
    rows, width = own.shape
    half = rows // 2
    weight[:, pl.ds(pl.multiple_of(me * width, 128), width)] = own[...]
    for step in range(1, seq_count):
        place = pl.ds(pl.multiple_of((me ^ step) * width, 128), width)
        weight[pl.ds(pl.multiple_of(part * half, 128), half), place] = mine[step - 1][...]
        weight[pl.ds(pl.multiple_of((1 - part) * half, 128), half), place] = theirs[step - 1][...]
    local, time_len, depth = cots[0].shape
    for r in range(band_count):
        block = [cots[r * seq_count + step][...].reshape(local * time_len, depth) for step in range(seq_count)]
        grad = nt_dot(jnp.concatenate(block, axis=0), weight[...]).astype(jnp.bfloat16)
        for head in range(rows // HD):
            lanes = slice(head * HD, (head + 1) * HD)
            back = nn_dot(probs_t[r, head], grad[:, lanes]).astype(jnp.bfloat16)
            back = back.reshape(seq_count, local, time_len, HD)
            for step in range(seq_count):
                outs[step][:, sub ^ r, :, lanes] = back[step]


def space_grad(ids, probs_t, own, mine, theirs, cots, seq_count, band_count):
    local, time_len, depth = cots[0].shape
    rows = own.shape[0]
    full = lambda array: pl.BlockSpec(array.shape, lambda i, ids: (0,) * array.ndim)
    operands = (probs_t, own, *mine, *theirs, *cots)
    out_shape = jax.ShapeDtypeStruct((local, band_count, time_len, rows), jnp.bfloat16)
    return pl.pallas_call(
        functools.partial(space_grad_kernel, seq_count=seq_count, band_count=band_count),
        grid_spec=pltpu.PrefetchScalarGridSpec(
            num_scalar_prefetch=1,
            grid=(1,),
            in_specs=[full(array) for array in operands],
            out_specs=[pl.BlockSpec(out_shape.shape, lambda i, ids: (0, 0, 0, 0))] * seq_count,
            scratch_shapes=[pltpu.VMEM((rows, depth), jnp.bfloat16)],
        ),
        out_shape=[out_shape] * seq_count,
        compiler_params=params(),
        name="space_grad",
    )(ids, *operands)


def space_backward_kernel(ids, q, k, v, probs, *rest):
    pieces, (dq, dk, dv, spare) = rest[:-4], rest[-4:]
    me = ids[0]
    for step, piece in enumerate(pieces):
        spare[:, me ^ step] = piece[0]
    upstream = spare[...].reshape(q.shape[1:])
    low = probs[0]
    dv[0] = nn_dot(low, upstream).astype(jnp.bfloat16)
    chance = nt_dot(v[0], upstream)
    wide = low.astype(jnp.float32)
    centre = jnp.sum(wide * chance, axis=0, keepdims=True)
    score = (wide * (chance - centre)).astype(jnp.bfloat16)
    dk[0] = (nn_dot(score, q[0]) * SCALE).astype(jnp.bfloat16)
    dq[0] = (tn_dot(k[0], score) * SCALE).T.astype(jnp.bfloat16)


def space_backward(ids, q, k, v, probs, pieces):
    frames, patches, columns = q.shape
    heads = columns // HD
    _, band_count, time_len, _ = pieces[0].shape
    wide = pl.BlockSpec((1, patches, HD), lambda f, h, ids: (f, 0, h))
    piece = pl.BlockSpec((1, band_count, time_len, HD), lambda f, h, ids: (f, 0, 0, h))
    square = pl.BlockSpec((1, patches, patches), lambda f, h, ids: (f * heads + h, 0, 0))
    return pl.pallas_call(
        space_backward_kernel,
        grid_spec=pltpu.PrefetchScalarGridSpec(
            num_scalar_prefetch=1,
            grid=(frames, heads),
            in_specs=[wide, wide, wide, square] + [piece] * len(pieces),
            out_specs=[wide, wide, wide],
            scratch_shapes=[pltpu.VMEM((band_count, len(pieces), time_len, HD), jnp.bfloat16)],
        ),
        out_shape=[jax.ShapeDtypeStruct(q.shape, jnp.bfloat16)] * 3,
        compiler_params=params(),
        name="space_backward",
    )(ids, q, k, v, probs, *pieces)


def on_small_slice(q_space, k_space, v_space, q_time, k_time, out_weight, cotangent):
    seq_count, band_count = lax.axis_size("seq"), lax.axis_size("sub")
    time_len = q_space.shape[1] // band_count // seq_count
    me, sub, part = lax.axis_index("seq"), lax.axis_index("sub"), lax.axis_index("parts")
    ids = jnp.stack([me, sub, part]).astype(jnp.int32)
    rows, width = out_weight.shape

    cot = [None] * seq_count
    for step in (2, 3, 1, 0):
        own = lax.dynamic_slice_in_dim(cotangent, (me ^ step) * time_len, time_len, 1)
        cot[step] = own if step == 0 else xor_send(own, "seq", step)
    half = lax.dynamic_slice_in_dim(out_weight, part * (rows // 2), rows // 2, 0)
    second = xor_send(half, "seq", 2)
    first = xor_send(half, "seq", 1)
    third = xor_send(second, "seq", 1)
    mine = [first, second, third]
    theirs = [swap_parts(piece) for piece in mine]
    bands = [cot, None, None, None]
    bands[2] = [xor_send(piece, "sub", 2) for piece in cot]
    bands[1] = [xor_send(piece, "sub", 1) for piece in cot]
    bands[3] = [xor_send(piece, "sub", 1) for piece in bands[2]]
    cots = [piece for band in bands for piece in band]

    pieces, probs = space_forward(ids, q_space, k_space, v_space, seq_count, band_count, time_len)
    moved = [pieces[0]] + [xor_send(pieces[step], "seq", step) for step in range(1, seq_count)]
    chances, chances_t = time_probs(ids, q_time, k_time, seq_count)

    back = space_grad(ids, chances_t, out_weight, mine, theirs, cots, seq_count, band_count)
    returned = [back[0]] + [xor_send(back[step], "seq", step) for step in range(1, seq_count)]

    mixed = time_out(ids, chances, moved).reshape(-1, rows)
    third_sum = weight_grad(ids, mixed, cots, 3, width, jnp.bfloat16)
    second_sum = weight_grad(ids, mixed, cots, 2, width, jnp.float32)
    first_sum = weight_grad(ids, mixed, cots, 1, width, jnp.bfloat16)
    own_sum = weight_grad(ids, mixed, cots, 0, width, jnp.float32)
    paired = (second_sum + xor_send(third_sum, "seq", 1).astype(jnp.float32)).astype(jnp.bfloat16)
    near = xor_send(first_sum, "seq", 1).astype(jnp.float32)
    far = xor_send(paired, "seq", 2).astype(jnp.float32)
    d_weight = own_sum + near + far

    dq, dk, dv = space_backward(ids, q_space, k_space, v_space, probs, returned)
    return dq, dk, dv, d_weight


def solution(mesh):
    in_specs = (
        P(("parts", "seq"), None, "sub"),
        P(("parts", "seq"), None, "sub"),
        P(("parts", "seq"), None, "sub"),
        P("parts", None, "seq", "sub"),
        P("parts", None, "seq", "sub"),
        P("sub", "seq"),
        P(("parts", "seq"), "sub", None),
    )
    out_specs = (
        P(("parts", "seq"), None, "sub"),
        P(("parts", "seq"), None, "sub"),
        P(("parts", "seq"), None, "sub"),
        P(("parts", "sub"), "seq"),
    )
    small = (mesh.shape["parts"], mesh.shape["seq"], mesh.shape["sub"]) == (2, 4, 4)
    return jax.shard_map(
        on_small_slice if small else on_device, mesh=mesh, in_specs=in_specs, out_specs=out_specs, check_vma=False
    )
```

```python
import functools
import math

import jax
import jax.numpy as jnp
from jax import lax
from jax.experimental import pallas as pl
from jax.experimental.pallas import tpu as pltpu
from jax.sharding import PartitionSpec as P

HD = 128
SCALE = 1.0 / math.sqrt(HD)


def normalize(scores):
    row_top = jnp.max(scores, axis=-1, keepdims=True)
    raised = jnp.exp(scores - row_top)
    return raised / jnp.sum(raised, axis=-1, keepdims=True)


def space_chances(query, keys):
    scores = jnp.einsum("fqhd,fkhd->fhqk", query, keys, preferred_element_type=jnp.float32) * (
        1.0 / math.sqrt(HD)
    )
    return normalize(scores)


def on_device(q_space, k_space, v_space, q_time, k_time, out_weight, cotangent):
    frame_count, patches, columns = q_space.shape
    head_count = columns // HD
    band_count = lax.axis_size("sub")
    seq_count = lax.axis_size("seq")
    all_frames = frame_count * seq_count
    band_len = patches // band_count
    time_len = band_len // seq_count
    split_shape = (frame_count, patches, head_count, HD)
    space_query = q_space.reshape(split_shape)
    space_keys = k_space.reshape(split_shape)
    space_values = v_space.reshape(split_shape)
    chances = space_chances(space_query, space_keys)
    space_out = jnp.einsum(
        "fhqk,fkhd->fqhd",
        chances.astype(jnp.bfloat16),
        space_values,
        preferred_element_type=jnp.float32,
    ).astype(jnp.bfloat16)
    moved = lax.all_to_all(
        space_out.reshape(frame_count, band_count, band_len, columns),
        "seq",
        split_axis=2,
        concat_axis=0,
        tiled=True,
    )
    time_shape = (all_frames, band_count, time_len, head_count, HD)
    time_query = q_time.reshape(time_shape)
    time_keys = k_time.reshape(time_shape)
    time_values = moved.reshape(time_shape)
    time_scores = jnp.einsum(
        "fbphd,gbphd->bphfg", time_query, time_keys, preferred_element_type=jnp.float32
    ) * (1.0 / math.sqrt(HD))
    time_chances = normalize(time_scores).astype(jnp.bfloat16)
    time_out = jnp.einsum(
        "bphfg,gbphd->fbphd", time_chances, time_values, preferred_element_type=jnp.float32
    ).astype(jnp.bfloat16)
    time_out = time_out.reshape(all_frames, band_count, time_len, columns)
    weight_rows = lax.all_gather(out_weight, "seq", axis=1, tiled=True)
    returned = lax.all_to_all(time_out, "seq", split_axis=0, concat_axis=2, tiled=True)
    frame_out = returned.reshape(frame_count, patches, columns)
    segment = lax.all_gather(cotangent, "sub", axis=1, tiled=True)
    weight_sum = jnp.einsum("fnh,fnd->hd", frame_out, segment, preferred_element_type=jnp.float32)
    update = jnp.einsum("fnd,hd->fnh", segment, weight_rows, preferred_element_type=jnp.float32)
    out_grad = update
    weight_sum, out_grad = (weight_sum, out_grad)
    rounded = out_grad.astype(jnp.bfloat16).reshape(frame_count, band_count, band_len, columns)
    time_grad = lax.all_to_all(rounded, "seq", split_axis=2, concat_axis=0, tiled=True)
    d_weight = lax.psum_scatter(
        weight_sum.astype(jnp.bfloat16), "seq", scatter_dimension=1, tiled=True
    ).astype(jnp.float32)
    value_time = jnp.einsum(
        "bphfg,fbphd->gbphd",
        time_chances,
        time_grad.reshape(time_shape),
        preferred_element_type=jnp.float32,
    ).astype(jnp.bfloat16)
    space_grad = lax.all_to_all(
        value_time.reshape(all_frames, band_count, time_len, columns),
        "seq",
        split_axis=0,
        concat_axis=2,
        tiled=True,
    )
    space_grad = space_grad.reshape(split_shape)
    recomputed = space_chances(space_query, space_keys)
    value_grad = jnp.einsum(
        "fhqk,fqhd->fkhd",
        recomputed.astype(jnp.bfloat16),
        space_grad,
        preferred_element_type=jnp.float32,
    ).astype(jnp.bfloat16)
    chance_grad = jnp.einsum(
        "fqhd,fkhd->fhqk", space_grad, space_values, preferred_element_type=jnp.float32
    )
    centre_term = jnp.sum(recomputed * chance_grad, axis=-1, keepdims=True)
    score_grad = (recomputed * (chance_grad - centre_term) * (1.0 / math.sqrt(HD))).astype(
        jnp.bfloat16
    )
    query_grad = jnp.einsum(
        "fhqk,fkhd->fqhd", score_grad, space_keys, preferred_element_type=jnp.float32
    ).astype(jnp.bfloat16)
    keys_grad = jnp.einsum(
        "fhqk,fqhd->fkhd", score_grad, space_query, preferred_element_type=jnp.float32
    ).astype(jnp.bfloat16)
    flat_shape = (frame_count, patches, columns)
    return (
        query_grad.reshape(flat_shape),
        keys_grad.reshape(flat_shape),
        value_grad.reshape(flat_shape),
        d_weight,
    )


def xor_send(value, axis, distance):
    count = lax.axis_size(axis)
    return lax.ppermute(value, axis, [(i, i ^ distance) for i in range(count)])


def trade(value):
    return lax.all_to_all(value, "seq", split_axis=0, concat_axis=0, tiled=True)


def swap_parts(value):
    return lax.ppermute(value, "parts", [(0, 1), (1, 0)])


def after(value, other):
    return lax.optimization_barrier((value, other))[0]


def nt_dot(a, b):
    return lax.dot_general(a, b, (((1,), (1,)), ((), ())), preferred_element_type=jnp.float32)


def tn_dot(a, b):
    return lax.dot_general(a, b, (((0,), (0,)), ((), ())), preferred_element_type=jnp.float32)


def nn_dot(a, b):
    return lax.dot_general(a, b, (((1,), (0,)), ((), ())), preferred_element_type=jnp.float32)


def softmax_rows(scores, scale, axis):
    raised = jnp.exp((scores - jnp.max(scores, axis=axis, keepdims=True)) * scale)
    return raised * (1.0 / jnp.sum(raised, axis=axis, keepdims=True))


def params():
    return pltpu.CompilerParams(vmem_limit_bytes=56 * 1024 * 1024)


def space_forward_kernel(q, k, v, out, probs):
    low = softmax_rows(nt_dot(k[0], q[0]), SCALE, 0).astype(jnp.bfloat16)
    probs[0] = low
    seq_count, _, band_count, time_len, _ = out.shape
    mixed = tn_dot(v[0], low).T.astype(jnp.bfloat16).reshape(band_count, seq_count, time_len, HD)
    for step in range(seq_count):
        out[step, 0] = mixed[:, step]


def space_forward(q, k, v, seq_count, band_count, time_len):
    frames, patches, columns = q.shape
    heads = columns // HD
    wide = pl.BlockSpec((1, patches, HD), lambda f, h: (f, 0, h))
    return pl.pallas_call(
        space_forward_kernel,
        grid=(frames, heads),
        in_specs=[wide, wide, wide],
        out_specs=[
            pl.BlockSpec((seq_count, 1, band_count, time_len, HD), lambda f, h: (0, f, 0, 0, h)),
            pl.BlockSpec((1, patches, patches), lambda f, h: (f * heads + h, 0, 0)),
        ],
        out_shape=[
            jax.ShapeDtypeStruct((seq_count, frames, band_count, time_len, columns), jnp.bfloat16),
            jax.ShapeDtypeStruct((frames * heads, patches, patches), jnp.bfloat16),
        ],
        compiler_params=params(),
        name="space_forward",
    )(q, k, v)


def time_probs_kernel(ids, q, k, probs_t, bias):
    frames, _, time_len, _ = q.shape
    rows = frames * time_len

    @pl.when((pl.program_id(0) == 0) & (pl.program_id(1) == 0))
    def _():
        place = [lax.broadcasted_iota(jnp.int32, (rows, rows), axis) % time_len for axis in (0, 1)]
        bias[...] = jnp.where(place[0] == place[1], 0.0, -1e30).astype(jnp.float32)

    scores = nt_dot(k[...].reshape(rows, HD), q[...].reshape(rows, HD)) + bias[...]
    probs_t[0, 0] = softmax_rows(scores, SCALE, 0).astype(jnp.bfloat16)


def time_probs(ids, q, k):
    frames, bands, time_len, columns = q.shape
    heads = columns // HD
    rows = frames * time_len
    spec = pl.BlockSpec((frames, 1, time_len, HD), lambda r, h, ids: (0, ids[1] ^ r, 0, h))
    return pl.pallas_call(
        time_probs_kernel,
        grid_spec=pltpu.PrefetchScalarGridSpec(
            num_scalar_prefetch=1,
            grid=(bands, heads),
            in_specs=[spec, spec],
            out_specs=pl.BlockSpec((1, 1, rows, rows), lambda r, h, ids: (r, h, 0, 0)),
            scratch_shapes=[pltpu.VMEM((rows, rows), jnp.float32)],
        ),
        out_shape=jax.ShapeDtypeStruct((bands, heads, rows, rows), jnp.bfloat16),
        compiler_params=params(),
        name="time_probs",
    )(ids, q, k)


def time_out_kernel(ids, probs_t, values, out):
    rows = probs_t.shape[2]
    for head in range(probs_t.shape[1]):
        lanes = slice(head * HD, (head + 1) * HD)
        own = values[:, :, 0, :, lanes].reshape(rows, HD)
        out[lanes, :] = tn_dot(own, probs_t[0, head]).astype(jnp.bfloat16)


def time_out(ids, probs_t, values):
    bands, heads, rows, _ = probs_t.shape
    seq_count, local, _, time_len, columns = values.shape
    return pl.pallas_call(
        time_out_kernel,
        grid_spec=pltpu.PrefetchScalarGridSpec(
            num_scalar_prefetch=1,
            grid=(bands,),
            in_specs=[
                pl.BlockSpec((1, heads, rows, rows), lambda r, ids: (r, 0, 0, 0)),
                pl.BlockSpec((seq_count, local, 1, time_len, columns), lambda r, ids: (0, 0, ids[1] ^ r, 0, 0)),
            ],
            out_specs=pl.BlockSpec((columns, rows), lambda r, ids: (0, r)),
        ),
        out_shape=jax.ShapeDtypeStruct((columns, bands * rows), jnp.bfloat16),
        compiler_params=params(),
        name="time_out",
    )(ids, probs_t, values)


def tokens_of(refs):
    sides = [jnp.concatenate([ref[...].reshape(-1, ref.shape[-1]) for ref in side], axis=0) for side in refs]
    return jnp.concatenate(sides, axis=1)


def weight_grad_kernel(ids, left, *rest):
    cots, out = rest[:-1], rest[-1]
    half = len(cots) // 2
    out[...] = nn_dot(left[...], tokens_of((cots[:half], cots[half:]))).astype(out.dtype)


def weight_grad(ids, left, cots, step, width, dtype):
    columns, tokens = left.shape
    cot_spec = pl.BlockSpec((*cots[0].shape[:2], width // 2), lambda i, ids: (0, 0, ids[0] ^ step))
    return pl.pallas_call(
        weight_grad_kernel,
        grid_spec=pltpu.PrefetchScalarGridSpec(
            num_scalar_prefetch=1,
            grid=(1,),
            in_specs=[pl.BlockSpec((columns, tokens), lambda i, ids: (0, 0))] + [cot_spec] * len(cots),
            out_specs=pl.BlockSpec((columns, width), lambda i, ids: (0, 0)),
        ),
        out_shape=jax.ShapeDtypeStruct((columns, width), dtype),
        compiler_params=params(),
        name="weight_grad",
    )(ids, left, *cots)


def space_grad_kernel(ids, probs_t, own, near, third, other_near, other_third, *rest, seq_count, band_count):
    cots, out, grad = rest[:-2], rest[-2], rest[-1]
    sub, part = ids[1], ids[2]
    rows = own.shape[0]
    half = rows // 2
    tokens = tokens_of((cots[:band_count], cots[band_count:]))

    def own_half(which):
        return own[pl.ds(pl.multiple_of(which * half, 128), half)]

    halves = (
        lambda: (own_half(part), own_half(1 - part)),
        lambda: (near[:half], other_near[:half]),
        lambda: (near[half:], other_near[half:]),
        lambda: (third[...], other_third[...]),
    )
    for step in range(seq_count):

        @pl.when(pl.program_id(0) == step)
        def _():
            grown = nt_dot(tokens, jnp.concatenate(halves[step](), axis=0))
            grad[...] = grown if step == 0 else grad[...] + grown

    frames, time_len, _ = cots[0].shape
    block, heads = grad.shape[0] // band_count, half // HD

    @pl.when(pl.program_id(0) == seq_count - 1)
    def _():
        for r in range(band_count):
            for place in range(2 * heads):
                head = (part ^ (place // heads)) * heads + place % heads
                lanes = pl.ds(pl.multiple_of(head * HD, HD), HD)
                low = grad[r * block : (r + 1) * block, place * HD : (place + 1) * HD].astype(jnp.bfloat16)
                back = nn_dot(probs_t[r, head], low).astype(jnp.bfloat16)
                out[:, :, sub ^ r, :, lanes] = back.reshape(seq_count, frames // seq_count, time_len, HD)


def space_grad(ids, probs_t, weights, cots, seq_count, band_count):
    frames, time_len, depth = cots[0].shape
    rows, width = weights[0].shape
    full = lambda array: pl.BlockSpec(array.shape, lambda i, ids: (0,) * array.ndim)
    cot_spec = pl.BlockSpec((frames, time_len, width // 2), lambda i, ids: (0, 0, ids[0] ^ i))
    out_shape = (seq_count, frames // seq_count, band_count, time_len, rows)
    return pl.pallas_call(
        functools.partial(space_grad_kernel, seq_count=seq_count, band_count=band_count),
        grid_spec=pltpu.PrefetchScalarGridSpec(
            num_scalar_prefetch=1,
            grid=(seq_count,),
            in_specs=[full(probs_t)] + [full(array) for array in weights] + [cot_spec] * len(cots),
            out_specs=pl.BlockSpec(out_shape, lambda i, ids: (0, 0, 0, 0, 0)),
            scratch_shapes=[pltpu.VMEM((frames * time_len * band_count, rows), jnp.float32)],
        ),
        out_shape=jax.ShapeDtypeStruct(out_shape, jnp.bfloat16),
        compiler_params=params(),
        name="space_grad",
    )(ids, probs_t, *weights, *cots)


def space_backward_kernel(q, k, v, probs, piece, dq, dk, dv, spare):
    for step in range(piece.shape[0]):
        spare[:, step] = piece[step, 0]
    upstream = spare[...].reshape(q.shape[1:])
    low = probs[0]
    dv[0] = nn_dot(low, upstream).astype(jnp.bfloat16)
    chance = nt_dot(v[0], upstream)
    wide = low.astype(jnp.float32)
    centre = jnp.sum(wide * chance, axis=0, keepdims=True)
    score = (wide * (chance - centre)).astype(jnp.bfloat16)
    dk[0] = (nn_dot(score, q[0]) * SCALE).astype(jnp.bfloat16)
    dq[0] = (tn_dot(k[0], score) * SCALE).T.astype(jnp.bfloat16)


def space_backward(q, k, v, probs, back):
    frames, patches, columns = q.shape
    heads = columns // HD
    seq_count, _, band_count, time_len, _ = back.shape
    wide = pl.BlockSpec((1, patches, HD), lambda f, h: (f, 0, h))
    piece = pl.BlockSpec((seq_count, 1, band_count, time_len, HD), lambda f, h: (0, f, 0, 0, h))
    square = pl.BlockSpec((1, patches, patches), lambda f, h: (f * heads + h, 0, 0))
    return pl.pallas_call(
        space_backward_kernel,
        grid=(frames, heads),
        in_specs=[wide, wide, wide, square, piece],
        out_specs=[wide, wide, wide],
        out_shape=[jax.ShapeDtypeStruct(q.shape, jnp.bfloat16)] * 3,
        scratch_shapes=[pltpu.VMEM((band_count, seq_count, time_len, HD), jnp.bfloat16)],
        compiler_params=params(),
        name="space_backward",
    )(q, k, v, probs, back)


def on_small_slice(q_space, k_space, v_space, q_time, k_time, out_weight, cotangent):
    seq_count, band_count = lax.axis_size("seq"), lax.axis_size("sub")
    time_len = q_space.shape[1] // band_count // seq_count
    me, sub, part = lax.axis_index("seq"), lax.axis_index("sub"), lax.axis_index("parts")
    ids = jnp.stack([me, sub, part]).astype(jnp.int32)
    rows, width = out_weight.shape

    local, depth = cotangent.shape[0], cotangent.shape[2]
    split = []
    for side in range(2):
        starts = [shard * width + side * (width // 2) for shard in range(seq_count)]
        picked = jnp.concatenate([cotangent[:, :, start : start + width // 2] for start in starts], axis=2)
        picked = picked.reshape(local, seq_count, time_len, depth // 2).transpose(1, 0, 2, 3)
        split.append(picked.reshape(seq_count * local, time_len, depth // 2))
    here = [trade(split[side]) for side in range(2)]
    q_space = after(q_space, split)
    mixed, probs = space_forward(q_space, k_space, v_space, seq_count, band_count, time_len)
    moved = trade(mixed)
    q_time = after(q_time, mixed)
    chances = time_probs(ids, q_time, k_time)
    here[1] = after(here[1], chances)
    cots = []
    for side in here:
        across = xor_send(side, "sub", 2)
        cots += [side, xor_send(side, "sub", 1), across, xor_send(across, "sub", 1)]

    half = lax.dynamic_slice_in_dim(out_weight, part * (rows // 2), rows // 2, 0)
    half = after(half, here[1])
    second = xor_send(half, "seq", 2)
    first = xor_send(half, "seq", 1)
    third = xor_send(second, "seq", 1)
    near_rows = jnp.concatenate([first, second], axis=0)
    weights = [out_weight, near_rows, third, swap_parts(near_rows), swap_parts(third)]
    returned = trade(space_grad(ids, chances, weights, cots, seq_count, band_count))

    turned = time_out(ids, chances, moved)
    third_sum = weight_grad(ids, turned, cots, 3, width, jnp.bfloat16)
    second_sum = weight_grad(ids, turned, cots, 2, width, jnp.float32)
    first_sum = weight_grad(ids, turned, cots, 1, width, jnp.bfloat16)
    own_sum = weight_grad(ids, turned, cots, 0, width, jnp.float32)
    paired = (second_sum + xor_send(third_sum, "seq", 1).astype(jnp.float32)).astype(jnp.bfloat16)
    near = xor_send(first_sum, "seq", 1).astype(jnp.float32)
    far = xor_send(paired, "seq", 2).astype(jnp.float32)
    d_weight = own_sum + near + far

    dq, dk, dv = space_backward(q_space, k_space, v_space, probs, returned)
    return dq, dk, dv, d_weight


def solution(mesh):
    in_specs = (
        P(("parts", "seq"), None, "sub"),
        P(("parts", "seq"), None, "sub"),
        P(("parts", "seq"), None, "sub"),
        P("parts", None, "seq", "sub"),
        P("parts", None, "seq", "sub"),
        P("sub", "seq"),
        P(("parts", "seq"), "sub", None),
    )
    out_specs = (
        P(("parts", "seq"), None, "sub"),
        P(("parts", "seq"), None, "sub"),
        P(("parts", "seq"), None, "sub"),
        P(("parts", "sub"), "seq"),
    )
    small = (mesh.shape["parts"], mesh.shape["seq"], mesh.shape["sub"]) == (2, 4, 4)
    return jax.shard_map(
        on_small_slice if small else on_device, mesh=mesh, in_specs=in_specs, out_specs=out_specs, check_vma=False
    )
```

```python
import functools
import math

import jax
import jax.numpy as jnp
from jax import lax
from jax.experimental import pallas as pl
from jax.experimental.pallas import tpu as pltpu
from jax.sharding import PartitionSpec as P

HD = 128
SCALE = 1.0 / math.sqrt(HD)


def normalize(scores):
    row_top = jnp.max(scores, axis=-1, keepdims=True)
    raised = jnp.exp(scores - row_top)
    return raised / jnp.sum(raised, axis=-1, keepdims=True)


def space_chances(query, keys):
    scores = jnp.einsum("fqhd,fkhd->fhqk", query, keys, preferred_element_type=jnp.float32) * (
        1.0 / math.sqrt(HD)
    )
    return normalize(scores)


def on_device(q_space, k_space, v_space, q_time, k_time, out_weight, cotangent):
    frame_count, patches, columns = q_space.shape
    head_count = columns // HD
    band_count = lax.axis_size("sub")
    seq_count = lax.axis_size("seq")
    all_frames = frame_count * seq_count
    band_len = patches // band_count
    time_len = band_len // seq_count
    split_shape = (frame_count, patches, head_count, HD)
    space_query = q_space.reshape(split_shape)
    space_keys = k_space.reshape(split_shape)
    space_values = v_space.reshape(split_shape)
    chances = space_chances(space_query, space_keys)
    space_out = jnp.einsum(
        "fhqk,fkhd->fqhd",
        chances.astype(jnp.bfloat16),
        space_values,
        preferred_element_type=jnp.float32,
    ).astype(jnp.bfloat16)
    moved = lax.all_to_all(
        space_out.reshape(frame_count, band_count, band_len, columns),
        "seq",
        split_axis=2,
        concat_axis=0,
        tiled=True,
    )
    time_shape = (all_frames, band_count, time_len, head_count, HD)
    time_query = q_time.reshape(time_shape)
    time_keys = k_time.reshape(time_shape)
    time_values = moved.reshape(time_shape)
    time_scores = jnp.einsum(
        "fbphd,gbphd->bphfg", time_query, time_keys, preferred_element_type=jnp.float32
    ) * (1.0 / math.sqrt(HD))
    time_chances = normalize(time_scores).astype(jnp.bfloat16)
    time_out = jnp.einsum(
        "bphfg,gbphd->fbphd", time_chances, time_values, preferred_element_type=jnp.float32
    ).astype(jnp.bfloat16)
    time_out = time_out.reshape(all_frames, band_count, time_len, columns)
    weight_rows = lax.all_gather(out_weight, "seq", axis=1, tiled=True)
    returned = lax.all_to_all(time_out, "seq", split_axis=0, concat_axis=2, tiled=True)
    frame_out = returned.reshape(frame_count, patches, columns)
    segment = lax.all_gather(cotangent, "sub", axis=1, tiled=True)
    weight_sum = jnp.einsum("fnh,fnd->hd", frame_out, segment, preferred_element_type=jnp.float32)
    update = jnp.einsum("fnd,hd->fnh", segment, weight_rows, preferred_element_type=jnp.float32)
    out_grad = update
    weight_sum, out_grad = (weight_sum, out_grad)
    rounded = out_grad.astype(jnp.bfloat16).reshape(frame_count, band_count, band_len, columns)
    time_grad = lax.all_to_all(rounded, "seq", split_axis=2, concat_axis=0, tiled=True)
    d_weight = lax.psum_scatter(
        weight_sum.astype(jnp.bfloat16), "seq", scatter_dimension=1, tiled=True
    ).astype(jnp.float32)
    value_time = jnp.einsum(
        "bphfg,fbphd->gbphd",
        time_chances,
        time_grad.reshape(time_shape),
        preferred_element_type=jnp.float32,
    ).astype(jnp.bfloat16)
    space_grad = lax.all_to_all(
        value_time.reshape(all_frames, band_count, time_len, columns),
        "seq",
        split_axis=0,
        concat_axis=2,
        tiled=True,
    )
    space_grad = space_grad.reshape(split_shape)
    recomputed = space_chances(space_query, space_keys)
    value_grad = jnp.einsum(
        "fhqk,fqhd->fkhd",
        recomputed.astype(jnp.bfloat16),
        space_grad,
        preferred_element_type=jnp.float32,
    ).astype(jnp.bfloat16)
    chance_grad = jnp.einsum(
        "fqhd,fkhd->fhqk", space_grad, space_values, preferred_element_type=jnp.float32
    )
    centre_term = jnp.sum(recomputed * chance_grad, axis=-1, keepdims=True)
    score_grad = (recomputed * (chance_grad - centre_term) * (1.0 / math.sqrt(HD))).astype(
        jnp.bfloat16
    )
    query_grad = jnp.einsum(
        "fhqk,fkhd->fqhd", score_grad, space_keys, preferred_element_type=jnp.float32
    ).astype(jnp.bfloat16)
    keys_grad = jnp.einsum(
        "fhqk,fqhd->fkhd", score_grad, space_query, preferred_element_type=jnp.float32
    ).astype(jnp.bfloat16)
    flat_shape = (frame_count, patches, columns)
    return (
        query_grad.reshape(flat_shape),
        keys_grad.reshape(flat_shape),
        value_grad.reshape(flat_shape),
        d_weight,
    )


def xor_send(value, axis, distance):
    count = lax.axis_size(axis)
    return lax.ppermute(value, axis, [(i, i ^ distance) for i in range(count)])


def trade(value):
    return lax.all_to_all(value, "seq", split_axis=0, concat_axis=0, tiled=True)


def swap_parts(value):
    return lax.ppermute(value, "parts", [(0, 1), (1, 0)])


def after(value, other):
    return lax.optimization_barrier((value, other))[0]


def gate(values, other):
    return lax.optimization_barrier((values, other))[0]


def nt_dot(a, b):
    return lax.dot_general(a, b, (((1,), (1,)), ((), ())), preferred_element_type=jnp.float32)


def tn_dot(a, b):
    return lax.dot_general(a, b, (((0,), (0,)), ((), ())), preferred_element_type=jnp.float32)


def nn_dot(a, b):
    return lax.dot_general(a, b, (((1,), (0,)), ((), ())), preferred_element_type=jnp.float32)


def softmax_rows(scores, scale, axis):
    raised = jnp.exp((scores - jnp.max(scores, axis=axis, keepdims=True)) * scale)
    return raised * (1.0 / jnp.sum(raised, axis=axis, keepdims=True))


def params():
    return pltpu.CompilerParams(vmem_limit_bytes=56 * 1024 * 1024)


def whole(*arrays):
    return [pl.BlockSpec(array.shape, lambda i, ids, rank=len(array.shape): (0,) * rank) for array in arrays]


PAIR = 2


def space_forward_kernel(q, k, v, out, probs):
    seq_count, _, band_count, time_len, _ = out.shape
    for head in range(PAIR):
        lanes = slice(head * HD, (head + 1) * HD)
        low = softmax_rows(nt_dot(k[0, :, lanes], q[0, :, lanes]), SCALE, 0).astype(jnp.bfloat16)
        probs[head] = low
        mixed = tn_dot(v[0, :, lanes], low).T.astype(jnp.bfloat16)
        mixed = mixed.reshape(band_count, seq_count, time_len, HD)
        for step in range(seq_count):
            out[step, 0, :, :, lanes] = mixed[:, step]


def space_forward(q, k, v, seq_count, band_count, time_len):
    frames, patches, columns = q.shape
    heads = columns // HD
    steps = heads // PAIR
    wide = pl.BlockSpec((1, patches, PAIR * HD), lambda f, h: (f, 0, h))
    return pl.pallas_call(
        space_forward_kernel,
        grid=(frames, steps),
        in_specs=[wide, wide, wide],
        out_specs=[
            pl.BlockSpec((seq_count, 1, band_count, time_len, PAIR * HD), lambda f, h: (0, f, 0, 0, h)),
            pl.BlockSpec((PAIR, patches, patches), lambda f, h: (f * steps + h, 0, 0)),
        ],
        out_shape=[
            jax.ShapeDtypeStruct((seq_count, frames, band_count, time_len, columns), jnp.bfloat16),
            jax.ShapeDtypeStruct((frames * heads, patches, patches), jnp.bfloat16),
        ],
        compiler_params=params(),
        name="space_forward",
    )(q, k, v)


def time_probs_kernel(ids, q, k, probs_t, bias):
    frames, _, time_len, columns = q.shape
    rows = frames * time_len

    @pl.when(pl.program_id(0) == 0)
    def _():
        place = [lax.broadcasted_iota(jnp.int32, (rows, rows), axis) % time_len for axis in (0, 1)]
        bias[...] = jnp.where(place[0] == place[1], 0.0, -1e30).astype(jnp.float32)

    for head in range(columns // HD):
        lanes = slice(head * HD, (head + 1) * HD)
        scores = nt_dot(k[:, 0, :, lanes].reshape(rows, HD), q[:, 0, :, lanes].reshape(rows, HD))
        probs_t[0, head] = softmax_rows(scores + bias[...], SCALE, 0).astype(jnp.bfloat16)


def time_probs(ids, q, k):
    frames, bands, time_len, columns = q.shape
    heads = columns // HD
    rows = frames * time_len
    spec = pl.BlockSpec((frames, 1, time_len, columns), lambda r, ids: (0, ids[1] ^ r, 0, 0))
    return pl.pallas_call(
        time_probs_kernel,
        grid_spec=pltpu.PrefetchScalarGridSpec(
            num_scalar_prefetch=1,
            grid=(bands,),
            in_specs=[spec, spec],
            out_specs=pl.BlockSpec((1, heads, rows, rows), lambda r, ids: (r, 0, 0, 0)),
            scratch_shapes=[pltpu.VMEM((rows, rows), jnp.float32)],
        ),
        out_shape=jax.ShapeDtypeStruct((bands, heads, rows, rows), jnp.bfloat16),
        compiler_params=params(),
        name="time_probs",
    )(ids, q, k)


def weight_grad_kernel(ids, left, *rest):
    cots, outs = rest[:-2], rest[-2:]
    half = len(cots) // 2
    for step, out in enumerate(outs):

        @pl.when(pl.program_id(0) == step)
        def _():
            start = 0
            for side in (cots[:half], cots[half:]):
                width = side[0].shape[-1]
                right = jnp.concatenate([ref[...].reshape(-1, width) for ref in side], axis=0)
                out[:, start : start + width] = nn_dot(left[...], right).astype(out.dtype)
                start += width


def weight_first_kernel(ids, probs_t, values, *rest):
    cots, (left, *outs) = rest[:-3], rest[-3:]
    bands, heads, rows, _ = probs_t.shape

    @pl.when(pl.program_id(0) == 0)
    def _():
        for r in range(bands):
            for head in range(heads):
                lanes = slice(head * HD, (head + 1) * HD)
                own = values[:, :, ids[1] ^ r, :, lanes].reshape(rows, HD)
                left[lanes, r * rows : (r + 1) * rows] = tn_dot(own, probs_t[r, head]).astype(jnp.bfloat16)

    weight_grad_kernel(ids, left, *cots, *outs)


def weight_parts(columns, cots, shards, steps, dtype):
    def place(i, ids):
        return 0, 0, ids[0] ^ jnp.where(i == 0, steps[0], steps[1])

    specs = [pl.BlockSpec((*piece.shape[:2], piece.shape[2] // shards), place) for piece in cots]
    width = (cots[0].shape[2] + cots[-1].shape[2]) // shards
    return specs, [jax.ShapeDtypeStruct((columns, width), dtype)] * 2


def weight_first(ids, probs_t, values, cots):
    bands, _, rows, _ = probs_t.shape
    columns = values.shape[-1]
    specs, sums = weight_parts(columns, cots, values.shape[0], (3, 1), jnp.bfloat16)
    out_shape = [jax.ShapeDtypeStruct((columns, bands * rows), jnp.bfloat16)] + sums
    return pl.pallas_call(
        weight_first_kernel,
        grid_spec=pltpu.PrefetchScalarGridSpec(
            num_scalar_prefetch=1, grid=(2,), in_specs=whole(probs_t, values) + specs, out_specs=whole(*out_shape)
        ),
        out_shape=out_shape,
        compiler_params=params(),
        name="weight_first",
    )(ids, probs_t, values, *cots)


def weight_second(ids, left, cots, shards):
    specs, sums = weight_parts(left.shape[0], cots, shards, (2, 0), jnp.float32)
    return pl.pallas_call(
        weight_grad_kernel,
        grid_spec=pltpu.PrefetchScalarGridSpec(
            num_scalar_prefetch=1, grid=(2,), in_specs=whole(left) + specs, out_specs=whole(*sums)
        ),
        out_shape=sums,
        compiler_params=params(),
        name="weight_second",
    )(ids, left, *cots)


def space_grad_kernel(ids, own, first, second, third, other_near, other_third, *rest):
    cots, (probs_t, out, *weight, tokens_a, tokens_b, chances, sems) = rest[:-8], rest[-8:]
    me, sub, part = ids[0], ids[1], ids[2]
    rows = own.shape[0]
    lines = rows // 2
    mine, theirs = [pl.ds(pl.multiple_of(which * lines, 128), lines) for which in (part, 1 - part)]
    copies = []

    def fetch(source, target):
        copies.append(pltpu.make_async_copy(source, target, sems.at[len(copies)]))
        copies[-1].start()
        return copies[-1]

    def fetch_rows(side, start, width):
        picked = slice(start, start + width)
        started = [fetch(own.at[:, picked], weight[side].at[:, pl.ds(pl.multiple_of(me * width, 128), width)])]
        for where, pieces in (
            (mine, (first, second, third)),
            (theirs, (other_near.at[:lines], other_near.at[lines:], other_third)),
        ):
            for step, piece in enumerate(pieces, 1):
                place = pl.ds(pl.multiple_of((me ^ step) * width, 128), width)
                started.append(fetch(piece.at[:, picked], weight[side].at[where, place]))
        return started

    bands, heads, block, _ = probs_t.shape
    seq_count, local, _, time_len, _ = out.shape
    widths = [ref.shape[-1] // seq_count for ref in (tokens_a, tokens_b)]
    near_side = fetch_rows(0, 0, widths[0]) + [fetch(cots[0], tokens_a.at[0])]
    far_side = fetch_rows(1, widths[0], widths[1])
    far_side += [fetch(cots[bands], tokens_b.at[0]), fetch(probs_t.at[0], chances.at[0])]
    later = [
        [
            fetch(cots[r], tokens_a.at[r]),
            fetch(cots[bands + r], tokens_b.at[r]),
            fetch(probs_t.at[r], chances.at[r]),
        ]
        for r in range(1, bands)
    ]
    for r in range(bands):
        for copy in near_side if r == 0 else later[r - 1]:
            copy.wait()
        grad = nt_dot(tokens_a[r].reshape(block, -1), weight[0][...])
        if r == 0:
            for copy in far_side:
                copy.wait()
        grad = (grad + nt_dot(tokens_b[r].reshape(block, -1), weight[1][...])).astype(jnp.bfloat16)
        for head in range(heads):
            lanes = slice(head * HD, (head + 1) * HD)
            back = nn_dot(chances[r, head], grad[:, lanes]).astype(jnp.bfloat16)
            out[:, :, sub ^ r, :, lanes] = back.reshape(seq_count, local, time_len, HD)


def space_grad(ids, probs_t, weights, cots, seq_count):
    frames, time_len, _ = cots[0].shape
    rows, bands = weights[0].shape[0], len(cots) // 2
    out_shape = jax.ShapeDtypeStruct((seq_count, frames // seq_count, bands, time_len, rows), jnp.bfloat16)
    depths = (cots[0].shape[2], cots[-1].shape[2])
    return pl.pallas_call(
        space_grad_kernel,
        grid_spec=pltpu.PrefetchScalarGridSpec(
            num_scalar_prefetch=1,
            grid=(1,),
            in_specs=[pl.BlockSpec(memory_space=pl.ANY)] * (len(weights) + len(cots) + 1),
            out_specs=whole(out_shape)[0],
            scratch_shapes=[pltpu.VMEM((rows, depth), jnp.bfloat16) for depth in depths]
            + [pltpu.VMEM((bands, frames, time_len, depth), jnp.bfloat16) for depth in depths]
            + [
                pltpu.VMEM(probs_t.shape, jnp.bfloat16),
                pltpu.SemaphoreType.DMA((2 * (2 * seq_count - 1) + 3 * bands,)),
            ],
        ),
        out_shape=out_shape,
        compiler_params=params(),
        name="space_grad",
    )(ids, *weights, *cots, probs_t)


def space_backward_kernel(q, k, v, probs, piece, dq, dk, dv, spare):
    for head in range(PAIR):
        lanes = slice(head * HD, (head + 1) * HD)
        for step in range(piece.shape[0]):
            spare[head, :, step] = piece[step, 0, :, :, lanes]
        upstream = spare[head].reshape(q.shape[1], HD)
        low = probs[head]
        dv[0, :, lanes] = nn_dot(low, upstream).astype(jnp.bfloat16)
        chance = nt_dot(v[0, :, lanes], upstream)
        wide = low.astype(jnp.float32)
        centre = jnp.sum(wide * chance, axis=0, keepdims=True)
        score = (wide * (chance - centre)).astype(jnp.bfloat16)
        dk[0, :, lanes] = (nn_dot(score, q[0, :, lanes]) * SCALE).astype(jnp.bfloat16)
        dq[0, :, lanes] = (tn_dot(k[0, :, lanes], score) * SCALE).T.astype(jnp.bfloat16)


def space_backward(q, k, v, probs, back):
    frames, patches, columns = q.shape
    steps = columns // HD // PAIR
    seq_count, _, band_count, time_len, _ = back.shape
    wide = pl.BlockSpec((1, patches, PAIR * HD), lambda f, h: (f, 0, h))
    piece = pl.BlockSpec((seq_count, 1, band_count, time_len, PAIR * HD), lambda f, h: (0, f, 0, 0, h))
    square = pl.BlockSpec((PAIR, patches, patches), lambda f, h: (f * steps + h, 0, 0))
    return pl.pallas_call(
        space_backward_kernel,
        grid=(frames, steps),
        in_specs=[wide, wide, wide, square, piece],
        out_specs=[wide, wide, wide],
        out_shape=[jax.ShapeDtypeStruct(q.shape, jnp.bfloat16)] * 3,
        scratch_shapes=[pltpu.VMEM((PAIR, band_count, seq_count, time_len, HD), jnp.bfloat16)],
        compiler_params=params(),
        name="space_backward",
    )(q, k, v, probs, back)


def on_small_slice(q_space, k_space, v_space, q_time, k_time, out_weight, cotangent):
    seq_count, band_count = lax.axis_size("seq"), lax.axis_size("sub")
    time_len = q_space.shape[1] // band_count // seq_count
    me, sub, part = lax.axis_index("seq"), lax.axis_index("sub"), lax.axis_index("parts")
    ids = jnp.stack([me, sub, part]).astype(jnp.int32)
    rows, width = out_weight.shape

    half = lax.dynamic_slice_in_dim(out_weight, part * (rows // 2), rows // 2, 0)
    second = xor_send(half, "seq", 2)
    first = xor_send(half, "seq", 1)

    local = cotangent.shape[0]
    bounds = (0, width // 3, width)
    split = []
    for low, high in zip(bounds, bounds[1:]):
        picked = [cotangent[:, :, shard * width + low : shard * width + high] for shard in range(seq_count)]
        picked = jnp.concatenate(picked, axis=2)
        picked = picked.reshape(local, seq_count, time_len, -1).transpose(1, 0, 2, 3)
        split.append(picked.reshape(seq_count * local, time_len, -1))
    here = [trade(split[0]), None]
    q_space = after(q_space, split)
    mixed, probs = space_forward(q_space, k_space, v_space, seq_count, band_count, time_len)
    q_time = after(q_time, mixed)
    chances = time_probs(ids, q_time, k_time)
    first, second, here[0], following, mixed = gate((first, second, here[0], split[1], mixed), chances)
    here[1] = trade(following)
    third = xor_send(second, "seq", 1)
    other_near = swap_parts(jnp.concatenate([first, second], axis=0))
    across = [xor_send(here[0], "sub", 2), None]
    beside = [xor_send(here[0], "sub", 1), None]

    here[1], third, other_near, across[0], mixed = gate((here[1], third, other_near, across[0], mixed), beside[0])
    moved = trade(mixed)
    across[1] = xor_send(here[1], "sub", 2)
    beside[1] = xor_send(here[1], "sub", 1)
    cross = [xor_send(across[0], "sub", 1), None]
    other_third = swap_parts(third)
    across[1] = after(across[1], (other_third, cross[0]))
    cross[1] = xor_send(across[1], "sub", 1)
    cots = []
    for side in range(2):
        cots += [here[side], beside[side], across[side], cross[side]]
    weights = [out_weight, first, second, third, other_near, other_third]

    turned, third_sum, first_sum = weight_first(ids, chances, moved, cots)
    back = space_grad(ids, after(chances, third_sum), weights, cots, seq_count)
    returned = trade(back)
    second_sum, own_sum = weight_second(ids, after(turned, back), cots, seq_count)
    third_sum = xor_send(third_sum, "seq", 1)
    paired = (second_sum + third_sum.astype(jnp.float32)).astype(jnp.bfloat16)
    far = xor_send(paired, "seq", 2)
    near = xor_send(after(first_sum, third_sum), "seq", 1)
    dq, dk, dv = space_backward(q_space, k_space, v_space, probs, returned)
    far, near = gate((far, near), dq)
    d_weight = own_sum + near.astype(jnp.float32) + far.astype(jnp.float32)
    return dq, dk, dv, d_weight


def solution(mesh):
    in_specs = (
        P(("parts", "seq"), None, "sub"),
        P(("parts", "seq"), None, "sub"),
        P(("parts", "seq"), None, "sub"),
        P("parts", None, "seq", "sub"),
        P("parts", None, "seq", "sub"),
        P("sub", "seq"),
        P(("parts", "seq"), "sub", None),
    )
    out_specs = (
        P(("parts", "seq"), None, "sub"),
        P(("parts", "seq"), None, "sub"),
        P(("parts", "seq"), None, "sub"),
        P(("parts", "sub"), "seq"),
    )
    small = (mesh.shape["parts"], mesh.shape["seq"], mesh.shape["sub"]) == (2, 4, 4)
    return jax.shard_map(
        on_small_slice if small else on_device, mesh=mesh, in_specs=in_specs, out_specs=out_specs, check_vma=False
    )
```

```python
import functools
import math

import jax
import jax.numpy as jnp
from jax import lax
from jax.experimental import pallas as pl
from jax.experimental.pallas import tpu as pltpu
from jax.sharding import PartitionSpec as P

HD = 128
SCALE = 1.0 / math.sqrt(HD)


def normalize(scores):
    row_top = jnp.max(scores, axis=-1, keepdims=True)
    raised = jnp.exp(scores - row_top)
    return raised / jnp.sum(raised, axis=-1, keepdims=True)


def space_chances(query, keys):
    scores = jnp.einsum("fqhd,fkhd->fhqk", query, keys, preferred_element_type=jnp.float32) * (
        1.0 / math.sqrt(HD)
    )
    return normalize(scores)


def on_device(q_space, k_space, v_space, q_time, k_time, out_weight, cotangent):
    frame_count, patches, columns = q_space.shape
    head_count = columns // HD
    band_count = lax.axis_size("sub")
    seq_count = lax.axis_size("seq")
    all_frames = frame_count * seq_count
    band_len = patches // band_count
    time_len = band_len // seq_count
    split_shape = (frame_count, patches, head_count, HD)
    space_query = q_space.reshape(split_shape)
    space_keys = k_space.reshape(split_shape)
    space_values = v_space.reshape(split_shape)
    chances = space_chances(space_query, space_keys)
    space_out = jnp.einsum(
        "fhqk,fkhd->fqhd",
        chances.astype(jnp.bfloat16),
        space_values,
        preferred_element_type=jnp.float32,
    ).astype(jnp.bfloat16)
    moved = lax.all_to_all(
        space_out.reshape(frame_count, band_count, band_len, columns),
        "seq",
        split_axis=2,
        concat_axis=0,
        tiled=True,
    )
    time_shape = (all_frames, band_count, time_len, head_count, HD)
    time_query = q_time.reshape(time_shape)
    time_keys = k_time.reshape(time_shape)
    time_values = moved.reshape(time_shape)
    time_scores = jnp.einsum(
        "fbphd,gbphd->bphfg", time_query, time_keys, preferred_element_type=jnp.float32
    ) * (1.0 / math.sqrt(HD))
    time_chances = normalize(time_scores).astype(jnp.bfloat16)
    time_out = jnp.einsum(
        "bphfg,gbphd->fbphd", time_chances, time_values, preferred_element_type=jnp.float32
    ).astype(jnp.bfloat16)
    time_out = time_out.reshape(all_frames, band_count, time_len, columns)
    weight_rows = lax.all_gather(out_weight, "seq", axis=1, tiled=True)
    returned = lax.all_to_all(time_out, "seq", split_axis=0, concat_axis=2, tiled=True)
    frame_out = returned.reshape(frame_count, patches, columns)
    segment = lax.all_gather(cotangent, "sub", axis=1, tiled=True)
    weight_sum = jnp.einsum("fnh,fnd->hd", frame_out, segment, preferred_element_type=jnp.float32)
    update = jnp.einsum("fnd,hd->fnh", segment, weight_rows, preferred_element_type=jnp.float32)
    out_grad = update
    weight_sum, out_grad = (weight_sum, out_grad)
    rounded = out_grad.astype(jnp.bfloat16).reshape(frame_count, band_count, band_len, columns)
    time_grad = lax.all_to_all(rounded, "seq", split_axis=2, concat_axis=0, tiled=True)
    d_weight = lax.psum_scatter(
        weight_sum.astype(jnp.bfloat16), "seq", scatter_dimension=1, tiled=True
    ).astype(jnp.float32)
    value_time = jnp.einsum(
        "bphfg,fbphd->gbphd",
        time_chances,
        time_grad.reshape(time_shape),
        preferred_element_type=jnp.float32,
    ).astype(jnp.bfloat16)
    space_grad = lax.all_to_all(
        value_time.reshape(all_frames, band_count, time_len, columns),
        "seq",
        split_axis=0,
        concat_axis=2,
        tiled=True,
    )
    space_grad = space_grad.reshape(split_shape)
    recomputed = space_chances(space_query, space_keys)
    value_grad = jnp.einsum(
        "fhqk,fqhd->fkhd",
        recomputed.astype(jnp.bfloat16),
        space_grad,
        preferred_element_type=jnp.float32,
    ).astype(jnp.bfloat16)
    chance_grad = jnp.einsum(
        "fqhd,fkhd->fhqk", space_grad, space_values, preferred_element_type=jnp.float32
    )
    centre_term = jnp.sum(recomputed * chance_grad, axis=-1, keepdims=True)
    score_grad = (recomputed * (chance_grad - centre_term) * (1.0 / math.sqrt(HD))).astype(
        jnp.bfloat16
    )
    query_grad = jnp.einsum(
        "fhqk,fkhd->fqhd", score_grad, space_keys, preferred_element_type=jnp.float32
    ).astype(jnp.bfloat16)
    keys_grad = jnp.einsum(
        "fhqk,fqhd->fkhd", score_grad, space_query, preferred_element_type=jnp.float32
    ).astype(jnp.bfloat16)
    flat_shape = (frame_count, patches, columns)
    return (
        query_grad.reshape(flat_shape),
        keys_grad.reshape(flat_shape),
        value_grad.reshape(flat_shape),
        d_weight,
    )


def xor_send(value, axis, distance):
    count = lax.axis_size(axis)
    return lax.ppermute(value, axis, [(i, i ^ distance) for i in range(count)])


def trade(value):
    return lax.all_to_all(value, "seq", split_axis=0, concat_axis=0, tiled=True)


def swap_parts(value):
    return lax.ppermute(value, "parts", [(0, 1), (1, 0)])


def after(value, other):
    return lax.optimization_barrier((value, other))[0]


def gate(values, other):
    return lax.optimization_barrier((values, other))[0]


def nt_dot(a, b):
    return lax.dot_general(a, b, (((1,), (1,)), ((), ())), preferred_element_type=jnp.float32)


def tn_dot(a, b):
    return lax.dot_general(a, b, (((0,), (0,)), ((), ())), preferred_element_type=jnp.float32)


def nn_dot(a, b):
    return lax.dot_general(a, b, (((1,), (0,)), ((), ())), preferred_element_type=jnp.float32)


def softmax_rows(scores, scale, axis):
    raised = jnp.exp((scores - jnp.max(scores, axis=axis, keepdims=True)) * scale)
    return raised * (1.0 / jnp.sum(raised, axis=axis, keepdims=True))


def params():
    return pltpu.CompilerParams(vmem_limit_bytes=56 * 1024 * 1024)


def whole(*arrays):
    return [pl.BlockSpec(array.shape, lambda i, ids, rank=len(array.shape): (0,) * rank) for array in arrays]


PAIR = 2


def space_forward_kernel(q, k, v, out, probs):
    seq_count, _, band_count, time_len, _ = out.shape
    for head in range(PAIR):
        lanes = slice(head * HD, (head + 1) * HD)
        low = softmax_rows(nt_dot(k[0, :, lanes], q[0, :, lanes]), SCALE, 0).astype(jnp.bfloat16)
        probs[head] = low
        mixed = tn_dot(v[0, :, lanes], low).T.astype(jnp.bfloat16)
        mixed = mixed.reshape(band_count, seq_count, time_len, HD)
        for step in range(seq_count):
            out[step, 0, :, :, lanes] = mixed[:, step]


def space_forward(q, k, v, seq_count, band_count, time_len):
    frames, patches, columns = q.shape
    heads = columns // HD
    steps = heads // PAIR
    wide = pl.BlockSpec((1, patches, PAIR * HD), lambda f, h: (f, 0, h))
    return pl.pallas_call(
        space_forward_kernel,
        grid=(frames, steps),
        in_specs=[wide, wide, wide],
        out_specs=[
            pl.BlockSpec((seq_count, 1, band_count, time_len, PAIR * HD), lambda f, h: (0, f, 0, 0, h)),
            pl.BlockSpec((PAIR, patches, patches), lambda f, h: (f * steps + h, 0, 0)),
        ],
        out_shape=[
            jax.ShapeDtypeStruct((seq_count, frames, band_count, time_len, columns), jnp.bfloat16),
            jax.ShapeDtypeStruct((frames * heads, patches, patches), jnp.bfloat16),
        ],
        compiler_params=params(),
        name="space_forward",
    )(q, k, v)


def time_probs_kernel(ids, q, k, probs_t, bias):
    frames, _, time_len, columns = q.shape
    rows = frames * time_len

    @pl.when(pl.program_id(0) == 0)
    def _():
        place = [lax.broadcasted_iota(jnp.int32, (rows, rows), axis) % time_len for axis in (0, 1)]
        bias[...] = jnp.where(place[0] == place[1], 0.0, -1e30).astype(jnp.float32)

    for head in range(columns // HD):
        lanes = slice(head * HD, (head + 1) * HD)
        scores = nt_dot(k[:, 0, :, lanes].reshape(rows, HD), q[:, 0, :, lanes].reshape(rows, HD))
        probs_t[0, head] = softmax_rows(scores + bias[...], SCALE, 0).astype(jnp.bfloat16)


def time_probs(ids, q, k):
    frames, bands, time_len, columns = q.shape
    heads = columns // HD
    rows = frames * time_len
    spec = pl.BlockSpec((frames, 1, time_len, columns), lambda r, ids: (0, ids[1] ^ r, 0, 0))
    return pl.pallas_call(
        time_probs_kernel,
        grid_spec=pltpu.PrefetchScalarGridSpec(
            num_scalar_prefetch=1,
            grid=(bands,),
            in_specs=[spec, spec],
            out_specs=pl.BlockSpec((1, heads, rows, rows), lambda r, ids: (r, 0, 0, 0)),
            scratch_shapes=[pltpu.VMEM((rows, rows), jnp.float32)],
        ),
        out_shape=jax.ShapeDtypeStruct((bands, heads, rows, rows), jnp.bfloat16),
        compiler_params=params(),
        name="time_probs",
    )(ids, q, k)


def weight_grad_kernel(ids, left, *rest, count):
    cots, outs = rest[:-count], rest[-count:]
    half = len(cots) // 2
    for step, out in enumerate(outs):

        @pl.when(pl.program_id(0) == step)
        def _():
            start = 0
            for side in (cots[:half], cots[half:]):
                width = side[0].shape[-1]
                right = jnp.concatenate([ref[...].reshape(-1, width) for ref in side], axis=0)
                out[:, start : start + width] = nn_dot(left[...], right).astype(out.dtype)
                start += width


def weight_first_kernel(ids, probs_t, values, *rest):
    cots, (left, out) = rest[:-2], rest[-2:]
    bands, heads, rows, _ = probs_t.shape

    @pl.when(pl.program_id(0) == 0)
    def _():
        for r in range(bands):
            for head in range(heads):
                lanes = slice(head * HD, (head + 1) * HD)
                own = values[:, :, ids[1] ^ r, :, lanes].reshape(rows, HD)
                left[lanes, r * rows : (r + 1) * rows] = tn_dot(own, probs_t[r, head]).astype(jnp.bfloat16)

    weight_grad_kernel(ids, left, *cots, out, count=1)


def weight_parts(columns, cots, shards, steps, dtypes):
    def place(i, ids):
        step = steps[0]
        for at, other in enumerate(steps[1:], 1):
            step = jnp.where(i == at, other, step)
        return 0, 0, ids[0] ^ step

    specs = [pl.BlockSpec((*piece.shape[:2], piece.shape[2] // shards), place) for piece in cots]
    width = (cots[0].shape[2] + cots[-1].shape[2]) // shards
    return specs, [jax.ShapeDtypeStruct((columns, width), dtype) for dtype in dtypes]


def weight_first(ids, probs_t, values, cots):
    bands, _, rows, _ = probs_t.shape
    columns = values.shape[-1]
    specs, sums = weight_parts(columns, cots, values.shape[0], (3,), (jnp.bfloat16,))
    out_shape = [jax.ShapeDtypeStruct((columns, bands * rows), jnp.bfloat16)] + sums
    return pl.pallas_call(
        weight_first_kernel,
        grid_spec=pltpu.PrefetchScalarGridSpec(
            num_scalar_prefetch=1, grid=(1,), in_specs=whole(probs_t, values) + specs, out_specs=whole(*out_shape)
        ),
        out_shape=out_shape,
        compiler_params=params(),
        name="weight_first",
    )(ids, probs_t, values, *cots)


def weight_second(ids, left, cots, shards):
    dtypes = (jnp.float32, jnp.float32, jnp.bfloat16)
    specs, sums = weight_parts(left.shape[0], cots, shards, (2, 0, 1), dtypes)
    return pl.pallas_call(
        functools.partial(weight_grad_kernel, count=3),
        grid_spec=pltpu.PrefetchScalarGridSpec(
            num_scalar_prefetch=1, grid=(3,), in_specs=whole(left) + specs, out_specs=whole(*sums)
        ),
        out_shape=sums,
        compiler_params=params(),
        name="weight_second",
    )(ids, left, *cots)


def space_grad_kernel(ids, own, first, second, third, other_near, other_third, *rest):
    cots, (probs_t, out, *weight, tokens_a, tokens_b, chances, sems) = rest[:-8], rest[-8:]
    me, sub, part = ids[0], ids[1], ids[2]
    rows = own.shape[0]
    lines = rows // 2
    mine, theirs = [pl.ds(pl.multiple_of(which * lines, 128), lines) for which in (part, 1 - part)]
    copies = []

    def fetch(source, target):
        copies.append(pltpu.make_async_copy(source, target, sems.at[len(copies)]))
        copies[-1].start()
        return copies[-1]

    def fetch_rows(side, start, width):
        picked = slice(start, start + width)
        started = [fetch(own.at[:, picked], weight[side].at[:, pl.ds(pl.multiple_of(me * width, 128), width)])]
        for where, pieces in (
            (mine, (first, second, third)),
            (theirs, (other_near.at[:lines], other_near.at[lines:], other_third)),
        ):
            for step, piece in enumerate(pieces, 1):
                place = pl.ds(pl.multiple_of((me ^ step) * width, 128), width)
                started.append(fetch(piece.at[:, picked], weight[side].at[where, place]))
        return started

    bands, heads, block, _ = probs_t.shape
    seq_count, local, _, time_len, _ = out.shape
    widths = [ref.shape[-1] // seq_count for ref in (tokens_a, tokens_b)]
    near_side = fetch_rows(0, 0, widths[0]) + [fetch(cots[0], tokens_a.at[0])]
    far_side = fetch_rows(1, widths[0], widths[1])
    far_side += [fetch(cots[bands], tokens_b.at[0]), fetch(probs_t.at[0], chances.at[0])]
    later = [
        [
            fetch(cots[r], tokens_a.at[r]),
            fetch(cots[bands + r], tokens_b.at[r]),
            fetch(probs_t.at[r], chances.at[r]),
        ]
        for r in range(1, bands)
    ]
    for r in range(bands):
        for copy in near_side if r == 0 else later[r - 1]:
            copy.wait()
        grad = nt_dot(tokens_a[r].reshape(block, -1), weight[0][...])
        if r == 0:
            for copy in far_side:
                copy.wait()
        grad = (grad + nt_dot(tokens_b[r].reshape(block, -1), weight[1][...])).astype(jnp.bfloat16)
        for head in range(heads):
            lanes = slice(head * HD, (head + 1) * HD)
            back = nn_dot(chances[r, head], grad[:, lanes]).astype(jnp.bfloat16)
            out[:, :, sub ^ r, :, lanes] = back.reshape(seq_count, local, time_len, HD)


def space_grad(ids, probs_t, weights, cots, seq_count):
    frames, time_len, _ = cots[0].shape
    rows, bands = weights[0].shape[0], len(cots) // 2
    out_shape = jax.ShapeDtypeStruct((seq_count, frames // seq_count, bands, time_len, rows), jnp.bfloat16)
    depths = (cots[0].shape[2], cots[-1].shape[2])
    return pl.pallas_call(
        space_grad_kernel,
        grid_spec=pltpu.PrefetchScalarGridSpec(
            num_scalar_prefetch=1,
            grid=(1,),
            in_specs=[pl.BlockSpec(memory_space=pl.ANY)] * (len(weights) + len(cots) + 1),
            out_specs=whole(out_shape)[0],
            scratch_shapes=[pltpu.VMEM((rows, depth), jnp.bfloat16) for depth in depths]
            + [pltpu.VMEM((bands, frames, time_len, depth), jnp.bfloat16) for depth in depths]
            + [
                pltpu.VMEM(probs_t.shape, jnp.bfloat16),
                pltpu.SemaphoreType.DMA((2 * (2 * seq_count - 1) + 3 * bands,)),
            ],
        ),
        out_shape=out_shape,
        compiler_params=params(),
        name="space_grad",
    )(ids, *weights, *cots, probs_t)


def space_backward_kernel(q, k, v, probs, piece, dq, dk, dv, spare):
    for head in range(PAIR):
        lanes = slice(head * HD, (head + 1) * HD)
        for step in range(piece.shape[0]):
            spare[head, :, step] = piece[step, 0, :, :, lanes]
        upstream = spare[head].reshape(q.shape[1], HD)
        low = probs[head]
        dv[0, :, lanes] = nn_dot(low, upstream).astype(jnp.bfloat16)
        chance = nt_dot(v[0, :, lanes], upstream)
        wide = low.astype(jnp.float32)
        centre = jnp.sum(wide * chance, axis=0, keepdims=True)
        score = (wide * (chance - centre)).astype(jnp.bfloat16)
        dk[0, :, lanes] = (nn_dot(score, q[0, :, lanes]) * SCALE).astype(jnp.bfloat16)
        dq[0, :, lanes] = (tn_dot(k[0, :, lanes], score) * SCALE).T.astype(jnp.bfloat16)


def space_backward(q, k, v, probs, back):
    frames, patches, columns = q.shape
    steps = columns // HD // PAIR
    seq_count, _, band_count, time_len, _ = back.shape
    wide = pl.BlockSpec((1, patches, PAIR * HD), lambda f, h: (f, 0, h))
    piece = pl.BlockSpec((seq_count, 1, band_count, time_len, PAIR * HD), lambda f, h: (0, f, 0, 0, h))
    square = pl.BlockSpec((PAIR, patches, patches), lambda f, h: (f * steps + h, 0, 0))
    return pl.pallas_call(
        space_backward_kernel,
        grid=(frames, steps),
        in_specs=[wide, wide, wide, square, piece],
        out_specs=[wide, wide, wide],
        out_shape=[jax.ShapeDtypeStruct(q.shape, jnp.bfloat16)] * 3,
        scratch_shapes=[pltpu.VMEM((PAIR, band_count, seq_count, time_len, HD), jnp.bfloat16)],
        compiler_params=params(),
        name="space_backward",
    )(q, k, v, probs, back)


def on_small_slice(q_space, k_space, v_space, q_time, k_time, out_weight, cotangent):
    seq_count, band_count = lax.axis_size("seq"), lax.axis_size("sub")
    time_len = q_space.shape[1] // band_count // seq_count
    me, sub, part = lax.axis_index("seq"), lax.axis_index("sub"), lax.axis_index("parts")
    ids = jnp.stack([me, sub, part]).astype(jnp.int32)
    rows, width = out_weight.shape

    half = lax.dynamic_slice_in_dim(out_weight, part * (rows // 2), rows // 2, 0)
    second = xor_send(half, "seq", 2)
    first = xor_send(half, "seq", 1)

    local = cotangent.shape[0]
    bounds = (0, width // 3, width)
    split = []
    for low, high in zip(bounds, bounds[1:]):
        picked = [cotangent[:, :, shard * width + low : shard * width + high] for shard in range(seq_count)]
        picked = jnp.concatenate(picked, axis=2)
        picked = picked.reshape(local, seq_count, time_len, -1).transpose(1, 0, 2, 3)
        split.append(picked.reshape(seq_count * local, time_len, -1))
    opening = split[0].reshape(seq_count, local, *split[0].shape[1:])
    opening = [lax.dynamic_index_in_dim(opening, me ^ step, 0, keepdims=False) for step in range(seq_count)]
    opening = [opening[0]] + [xor_send(opening[step], "seq", step) for step in range(1, seq_count)]
    q_space = after(q_space, split)
    mixed, probs = space_forward(q_space, k_space, v_space, seq_count, band_count, time_len)
    q_time = after(q_time, mixed)
    chances = time_probs(ids, q_time, k_time)
    first, second, opening, following, mixed = gate((first, second, opening, split[1], mixed), chances)
    here = [jnp.zeros_like(split[0]), trade(following)]
    for step in range(seq_count):
        here[0] = lax.dynamic_update_slice_in_dim(here[0], opening[step], (me ^ step) * local, 0)
    other_near = swap_parts(jnp.concatenate([first, second], axis=0))
    across = [xor_send(here[0], "sub", 2), None]
    beside = [xor_send(here[0], "sub", 1), None]

    gated = gate((here[1], second, other_near, across[0], mixed), beside[0])
    here[1], second, other_near, across[0], mixed = gated
    moved = trade(mixed)
    third = xor_send(second, "seq", 1)
    across[1] = xor_send(here[1], "sub", 2)
    beside[1] = xor_send(here[1], "sub", 1)
    cross = [xor_send(across[0], "sub", 1), None]
    other_third = swap_parts(third)
    across[1] = after(across[1], (other_third, cross[0]))
    cross[1] = xor_send(across[1], "sub", 1)
    cots = []
    for side in range(2):
        cots += [here[side], beside[side], across[side], cross[side]]
    weights = [out_weight, first, second, third, other_near, other_third]

    turned, third_sum = weight_first(ids, chances, moved, cots)
    back = space_grad(ids, after(chances, third_sum), weights, cots, seq_count)
    returned = trade(back)
    second_sum, own_sum, first_sum = weight_second(ids, after(turned, back), cots, seq_count)
    third_sum = xor_send(third_sum, "seq", 1)
    paired = (second_sum + third_sum.astype(jnp.float32)).astype(jnp.bfloat16)
    far = xor_send(paired, "seq", 2)
    near = xor_send(after(first_sum, third_sum), "seq", 1)
    dq, dk, dv = space_backward(q_space, k_space, v_space, probs, returned)
    far, near = gate((far, near), dq)
    d_weight = own_sum + near.astype(jnp.float32) + far.astype(jnp.float32)
    return dq, dk, dv, d_weight


def solution(mesh):
    in_specs = (
        P(("parts", "seq"), None, "sub"),
        P(("parts", "seq"), None, "sub"),
        P(("parts", "seq"), None, "sub"),
        P("parts", None, "seq", "sub"),
        P("parts", None, "seq", "sub"),
        P("sub", "seq"),
        P(("parts", "seq"), "sub", None),
    )
    out_specs = (
        P(("parts", "seq"), None, "sub"),
        P(("parts", "seq"), None, "sub"),
        P(("parts", "seq"), None, "sub"),
        P(("parts", "sub"), "seq"),
    )
    small = (mesh.shape["parts"], mesh.shape["seq"], mesh.shape["sub"]) == (2, 4, 4)
    return jax.shard_map(
        on_small_slice if small else on_device, mesh=mesh, in_specs=in_specs, out_specs=out_specs, check_vma=False
    )
```

```python
import functools
import math

import jax
import jax.numpy as jnp
from jax import lax
from jax.experimental import pallas as pl
from jax.experimental.pallas import tpu as pltpu
from jax.sharding import PartitionSpec as P

HD = 128
SCALE = 1.0 / math.sqrt(HD)


def normalize(scores):
    row_top = jnp.max(scores, axis=-1, keepdims=True)
    raised = jnp.exp(scores - row_top)
    return raised / jnp.sum(raised, axis=-1, keepdims=True)


def space_chances(query, keys):
    scores = jnp.einsum("fqhd,fkhd->fhqk", query, keys, preferred_element_type=jnp.float32) * (
        1.0 / math.sqrt(HD)
    )
    return normalize(scores)


def on_device(q_space, k_space, v_space, q_time, k_time, out_weight, cotangent):
    frame_count, patches, columns = q_space.shape
    head_count = columns // HD
    band_count = lax.axis_size("sub")
    seq_count = lax.axis_size("seq")
    all_frames = frame_count * seq_count
    band_len = patches // band_count
    time_len = band_len // seq_count
    split_shape = (frame_count, patches, head_count, HD)
    space_query = q_space.reshape(split_shape)
    space_keys = k_space.reshape(split_shape)
    space_values = v_space.reshape(split_shape)
    chances = space_chances(space_query, space_keys)
    space_out = jnp.einsum(
        "fhqk,fkhd->fqhd",
        chances.astype(jnp.bfloat16),
        space_values,
        preferred_element_type=jnp.float32,
    ).astype(jnp.bfloat16)
    moved = lax.all_to_all(
        space_out.reshape(frame_count, band_count, band_len, columns),
        "seq",
        split_axis=2,
        concat_axis=0,
        tiled=True,
    )
    time_shape = (all_frames, band_count, time_len, head_count, HD)
    time_query = q_time.reshape(time_shape)
    time_keys = k_time.reshape(time_shape)
    time_values = moved.reshape(time_shape)
    time_scores = jnp.einsum(
        "fbphd,gbphd->bphfg", time_query, time_keys, preferred_element_type=jnp.float32
    ) * (1.0 / math.sqrt(HD))
    time_chances = normalize(time_scores).astype(jnp.bfloat16)
    time_out = jnp.einsum(
        "bphfg,gbphd->fbphd", time_chances, time_values, preferred_element_type=jnp.float32
    ).astype(jnp.bfloat16)
    time_out = time_out.reshape(all_frames, band_count, time_len, columns)
    weight_rows = lax.all_gather(out_weight, "seq", axis=1, tiled=True)
    returned = lax.all_to_all(time_out, "seq", split_axis=0, concat_axis=2, tiled=True)
    frame_out = returned.reshape(frame_count, patches, columns)
    segment = lax.all_gather(cotangent, "sub", axis=1, tiled=True)
    weight_sum = jnp.einsum("fnh,fnd->hd", frame_out, segment, preferred_element_type=jnp.float32)
    update = jnp.einsum("fnd,hd->fnh", segment, weight_rows, preferred_element_type=jnp.float32)
    out_grad = update
    weight_sum, out_grad = (weight_sum, out_grad)
    rounded = out_grad.astype(jnp.bfloat16).reshape(frame_count, band_count, band_len, columns)
    time_grad = lax.all_to_all(rounded, "seq", split_axis=2, concat_axis=0, tiled=True)
    d_weight = lax.psum_scatter(
        weight_sum.astype(jnp.bfloat16), "seq", scatter_dimension=1, tiled=True
    ).astype(jnp.float32)
    value_time = jnp.einsum(
        "bphfg,fbphd->gbphd",
        time_chances,
        time_grad.reshape(time_shape),
        preferred_element_type=jnp.float32,
    ).astype(jnp.bfloat16)
    space_grad = lax.all_to_all(
        value_time.reshape(all_frames, band_count, time_len, columns),
        "seq",
        split_axis=0,
        concat_axis=2,
        tiled=True,
    )
    space_grad = space_grad.reshape(split_shape)
    recomputed = space_chances(space_query, space_keys)
    value_grad = jnp.einsum(
        "fhqk,fqhd->fkhd",
        recomputed.astype(jnp.bfloat16),
        space_grad,
        preferred_element_type=jnp.float32,
    ).astype(jnp.bfloat16)
    chance_grad = jnp.einsum(
        "fqhd,fkhd->fhqk", space_grad, space_values, preferred_element_type=jnp.float32
    )
    centre_term = jnp.sum(recomputed * chance_grad, axis=-1, keepdims=True)
    score_grad = (recomputed * (chance_grad - centre_term) * (1.0 / math.sqrt(HD))).astype(
        jnp.bfloat16
    )
    query_grad = jnp.einsum(
        "fhqk,fkhd->fqhd", score_grad, space_keys, preferred_element_type=jnp.float32
    ).astype(jnp.bfloat16)
    keys_grad = jnp.einsum(
        "fhqk,fqhd->fkhd", score_grad, space_query, preferred_element_type=jnp.float32
    ).astype(jnp.bfloat16)
    flat_shape = (frame_count, patches, columns)
    return (
        query_grad.reshape(flat_shape),
        keys_grad.reshape(flat_shape),
        value_grad.reshape(flat_shape),
        d_weight,
    )


def xor_send(value, axis, distance):
    count = lax.axis_size(axis)
    return lax.ppermute(value, axis, [(i, i ^ distance) for i in range(count)])


def trade(value):
    return lax.all_to_all(value, "seq", split_axis=0, concat_axis=0, tiled=True)


def swap_parts(value):
    return lax.ppermute(value, "parts", [(0, 1), (1, 0)])


def after(value, other):
    return lax.optimization_barrier((value, other))[0]


def gate(values, other):
    return lax.optimization_barrier((values, other))[0]


def nt_dot(a, b):
    return lax.dot_general(a, b, (((1,), (1,)), ((), ())), preferred_element_type=jnp.float32)


def tn_dot(a, b):
    return lax.dot_general(a, b, (((0,), (0,)), ((), ())), preferred_element_type=jnp.float32)


def nn_dot(a, b):
    return lax.dot_general(a, b, (((1,), (0,)), ((), ())), preferred_element_type=jnp.float32)


def softmax_rows(scores, scale, axis):
    raised = jnp.exp((scores - jnp.max(scores, axis=axis, keepdims=True)) * scale)
    return raised * (1.0 / jnp.sum(raised, axis=axis, keepdims=True))


def params():
    return pltpu.CompilerParams(vmem_limit_bytes=56 * 1024 * 1024)


def whole(*arrays):
    return [pl.BlockSpec(array.shape, lambda i, ids, rank=len(array.shape): (0,) * rank) for array in arrays]


PAIR = 2


def space_forward_kernel(q, k, v, out, probs):
    seq_count, _, band_count, time_len, _ = out.shape
    for head in range(PAIR):
        lanes = slice(head * HD, (head + 1) * HD)
        low = softmax_rows(nt_dot(k[0, :, lanes], q[0, :, lanes]), SCALE, 0).astype(jnp.bfloat16)
        probs[head] = low
        mixed = tn_dot(v[0, :, lanes], low).T.astype(jnp.bfloat16)
        mixed = mixed.reshape(band_count, seq_count, time_len, HD)
        for step in range(seq_count):
            out[step, 0, :, :, lanes] = mixed[:, step]


def space_forward(q, k, v, seq_count, band_count, time_len):
    frames, patches, columns = q.shape
    heads = columns // HD
    steps = heads // PAIR
    wide = pl.BlockSpec((1, patches, PAIR * HD), lambda f, h: (f, 0, h))
    return pl.pallas_call(
        space_forward_kernel,
        grid=(frames, steps),
        in_specs=[wide, wide, wide],
        out_specs=[
            pl.BlockSpec((seq_count, 1, band_count, time_len, PAIR * HD), lambda f, h: (0, f, 0, 0, h)),
            pl.BlockSpec((PAIR, patches, patches), lambda f, h: (f * steps + h, 0, 0)),
        ],
        out_shape=[
            jax.ShapeDtypeStruct((seq_count, frames, band_count, time_len, columns), jnp.bfloat16),
            jax.ShapeDtypeStruct((frames * heads, patches, patches), jnp.bfloat16),
        ],
        compiler_params=params(),
        name="space_forward",
    )(q, k, v)


def time_probs_kernel(ids, q, k, probs_t, bias):
    frames, _, time_len, columns = q.shape
    rows = frames * time_len

    @pl.when(pl.program_id(0) == 0)
    def _():
        place = [lax.broadcasted_iota(jnp.int32, (rows, rows), axis) % time_len for axis in (0, 1)]
        bias[...] = jnp.where(place[0] == place[1], 0.0, -1e30).astype(jnp.float32)

    for head in range(columns // HD):
        lanes = slice(head * HD, (head + 1) * HD)
        scores = nt_dot(k[:, 0, :, lanes].reshape(rows, HD), q[:, 0, :, lanes].reshape(rows, HD))
        probs_t[0, head] = softmax_rows(scores + bias[...], SCALE, 0).astype(jnp.bfloat16)


def time_probs(ids, q, k):
    frames, bands, time_len, columns = q.shape
    heads = columns // HD
    rows = frames * time_len
    spec = pl.BlockSpec((frames, 1, time_len, columns), lambda r, ids: (0, ids[1] ^ r, 0, 0))
    return pl.pallas_call(
        time_probs_kernel,
        grid_spec=pltpu.PrefetchScalarGridSpec(
            num_scalar_prefetch=1,
            grid=(bands,),
            in_specs=[spec, spec],
            out_specs=pl.BlockSpec((1, heads, rows, rows), lambda r, ids: (r, 0, 0, 0)),
            scratch_shapes=[pltpu.VMEM((rows, rows), jnp.float32)],
        ),
        out_shape=jax.ShapeDtypeStruct((bands, heads, rows, rows), jnp.bfloat16),
        compiler_params=params(),
        name="time_probs",
    )(ids, q, k)


def in_order_kernel(ids, *rest):
    pieces, out = rest[:-1], rest[-1]
    local = pieces[0].shape[0]
    for step, piece in enumerate(pieces):
        out[pl.ds((ids[0] ^ step) * local, local)] = piece[...]


def in_order(ids, pieces):
    local, *inner = pieces[0].shape
    out_shape = jax.ShapeDtypeStruct((len(pieces) * local, *inner), pieces[0].dtype)
    return pl.pallas_call(
        in_order_kernel,
        grid_spec=pltpu.PrefetchScalarGridSpec(
            num_scalar_prefetch=1, grid=(1,), in_specs=whole(*pieces), out_specs=whole(out_shape)[0]
        ),
        out_shape=out_shape,
        compiler_params=params(),
        name="in_order",
    )(ids, *pieces)


def weight_grad_kernel(ids, left, *rest, count):
    cots, outs = rest[:-count], rest[-count:]
    half = len(cots) // 2
    for step, out in enumerate(outs):

        @pl.when(pl.program_id(0) == step)
        def _():
            start = 0
            for side in (cots[:half], cots[half:]):
                width = side[0].shape[-1]
                right = jnp.concatenate([ref[...].reshape(-1, width) for ref in side], axis=0)
                out[:, start : start + width] = nn_dot(left[...], right).astype(out.dtype)
                start += width


def weight_first_kernel(ids, probs_t, values, *rest):
    cots, (left, out) = rest[:-2], rest[-2:]
    bands, heads, rows, _ = probs_t.shape

    @pl.when(pl.program_id(0) == 0)
    def _():
        for r in range(bands):
            for head in range(heads):
                lanes = slice(head * HD, (head + 1) * HD)
                own = values[:, :, ids[1] ^ r, :, lanes].reshape(rows, HD)
                left[lanes, r * rows : (r + 1) * rows] = tn_dot(own, probs_t[r, head]).astype(jnp.bfloat16)

    weight_grad_kernel(ids, left, *cots, out, count=1)


def weight_parts(columns, cots, shards, steps, dtypes):
    def place(i, ids):
        step = steps[0]
        for at, other in enumerate(steps[1:], 1):
            step = jnp.where(i == at, other, step)
        return 0, 0, ids[0] ^ step

    specs = [pl.BlockSpec((*piece.shape[:2], piece.shape[2] // shards), place) for piece in cots]
    width = (cots[0].shape[2] + cots[-1].shape[2]) // shards
    return specs, [jax.ShapeDtypeStruct((columns, width), dtype) for dtype in dtypes]


def weight_first(ids, probs_t, values, cots):
    bands, _, rows, _ = probs_t.shape
    columns = values.shape[-1]
    specs, sums = weight_parts(columns, cots, values.shape[0], (3,), (jnp.bfloat16,))
    out_shape = [jax.ShapeDtypeStruct((columns, bands * rows), jnp.bfloat16)] + sums
    return pl.pallas_call(
        weight_first_kernel,
        grid_spec=pltpu.PrefetchScalarGridSpec(
            num_scalar_prefetch=1, grid=(1,), in_specs=whole(probs_t, values) + specs, out_specs=whole(*out_shape)
        ),
        out_shape=out_shape,
        compiler_params=params(),
        name="weight_first",
    )(ids, probs_t, values, *cots)


def weight_second(ids, left, cots, shards):
    dtypes = (jnp.float32, jnp.float32, jnp.bfloat16)
    specs, sums = weight_parts(left.shape[0], cots, shards, (2, 0, 1), dtypes)
    return pl.pallas_call(
        functools.partial(weight_grad_kernel, count=3),
        grid_spec=pltpu.PrefetchScalarGridSpec(
            num_scalar_prefetch=1, grid=(3,), in_specs=whole(left) + specs, out_specs=whole(*sums)
        ),
        out_shape=sums,
        compiler_params=params(),
        name="weight_second",
    )(ids, left, *cots)


def space_grad_kernel(ids, own, first, second, third, other_near, other_third, *rest):
    cots, (probs_t, out, *weight, tokens_a, tokens_b, chances, sems) = rest[:-8], rest[-8:]
    me, sub, part = ids[0], ids[1], ids[2]
    rows = own.shape[0]
    lines = rows // 2
    mine, theirs = [pl.ds(pl.multiple_of(which * lines, 128), lines) for which in (part, 1 - part)]
    copies = []

    def fetch(source, target):
        copies.append(pltpu.make_async_copy(source, target, sems.at[len(copies)]))
        copies[-1].start()
        return copies[-1]

    def fetch_rows(side, start, width):
        picked = slice(start, start + width)
        started = [fetch(own.at[:, picked], weight[side].at[:, pl.ds(pl.multiple_of(me * width, 128), width)])]
        for where, pieces in (
            (mine, (first, second, third)),
            (theirs, (other_near.at[:lines], other_near.at[lines:], other_third)),
        ):
            for step, piece in enumerate(pieces, 1):
                place = pl.ds(pl.multiple_of((me ^ step) * width, 128), width)
                started.append(fetch(piece.at[:, picked], weight[side].at[where, place]))
        return started

    bands, heads, block, _ = probs_t.shape
    seq_count, local, _, time_len, _ = out.shape
    widths = [ref.shape[-1] // seq_count for ref in (tokens_a, tokens_b)]
    near_side = fetch_rows(0, 0, widths[0]) + [fetch(cots[0], tokens_a.at[0])]
    far_side = fetch_rows(1, widths[0], widths[1])
    far_side += [fetch(cots[bands], tokens_b.at[0]), fetch(probs_t.at[0], chances.at[0])]
    later = [
        [
            fetch(cots[r], tokens_a.at[r]),
            fetch(cots[bands + r], tokens_b.at[r]),
            fetch(probs_t.at[r], chances.at[r]),
        ]
        for r in range(1, bands)
    ]
    for r in range(bands):
        for copy in near_side if r == 0 else later[r - 1]:
            copy.wait()
        grad = nt_dot(tokens_a[r].reshape(block, -1), weight[0][...])
        if r == 0:
            for copy in far_side:
                copy.wait()
        grad = (grad + nt_dot(tokens_b[r].reshape(block, -1), weight[1][...])).astype(jnp.bfloat16)
        for head in range(heads):
            lanes = slice(head * HD, (head + 1) * HD)
            back = nn_dot(chances[r, head], grad[:, lanes]).astype(jnp.bfloat16)
            out[:, :, sub ^ r, :, lanes] = back.reshape(seq_count, local, time_len, HD)


def space_grad(ids, probs_t, weights, cots, seq_count):
    frames, time_len, _ = cots[0].shape
    rows, bands = weights[0].shape[0], len(cots) // 2
    out_shape = jax.ShapeDtypeStruct((seq_count, frames // seq_count, bands, time_len, rows), jnp.bfloat16)
    depths = (cots[0].shape[2], cots[-1].shape[2])
    return pl.pallas_call(
        space_grad_kernel,
        grid_spec=pltpu.PrefetchScalarGridSpec(
            num_scalar_prefetch=1,
            grid=(1,),
            in_specs=[pl.BlockSpec(memory_space=pl.ANY)] * (len(weights) + len(cots) + 1),
            out_specs=whole(out_shape)[0],
            scratch_shapes=[pltpu.VMEM((rows, depth), jnp.bfloat16) for depth in depths]
            + [pltpu.VMEM((bands, frames, time_len, depth), jnp.bfloat16) for depth in depths]
            + [
                pltpu.VMEM(probs_t.shape, jnp.bfloat16),
                pltpu.SemaphoreType.DMA((2 * (2 * seq_count - 1) + 3 * bands,)),
            ],
        ),
        out_shape=out_shape,
        compiler_params=params(),
        name="space_grad",
    )(ids, *weights, *cots, probs_t)


def space_backward_kernel(q, k, v, probs, piece, dq, dk, dv, spare):
    for head in range(PAIR):
        lanes = slice(head * HD, (head + 1) * HD)
        for step in range(piece.shape[0]):
            spare[head, :, step] = piece[step, 0, :, :, lanes]
        upstream = spare[head].reshape(q.shape[1], HD)
        low = probs[head]
        dv[0, :, lanes] = nn_dot(low, upstream).astype(jnp.bfloat16)
        chance = nt_dot(v[0, :, lanes], upstream)
        wide = low.astype(jnp.float32)
        centre = jnp.sum(wide * chance, axis=0, keepdims=True)
        score = (wide * (chance - centre)).astype(jnp.bfloat16)
        dk[0, :, lanes] = (nn_dot(score, q[0, :, lanes]) * SCALE).astype(jnp.bfloat16)
        dq[0, :, lanes] = (tn_dot(k[0, :, lanes], score) * SCALE).T.astype(jnp.bfloat16)


def space_backward(q, k, v, probs, back):
    frames, patches, columns = q.shape
    steps = columns // HD // PAIR
    seq_count, _, band_count, time_len, _ = back.shape
    wide = pl.BlockSpec((1, patches, PAIR * HD), lambda f, h: (f, 0, h))
    piece = pl.BlockSpec((seq_count, 1, band_count, time_len, PAIR * HD), lambda f, h: (0, f, 0, 0, h))
    square = pl.BlockSpec((PAIR, patches, patches), lambda f, h: (f * steps + h, 0, 0))
    return pl.pallas_call(
        space_backward_kernel,
        grid=(frames, steps),
        in_specs=[wide, wide, wide, square, piece],
        out_specs=[wide, wide, wide],
        out_shape=[jax.ShapeDtypeStruct(q.shape, jnp.bfloat16)] * 3,
        scratch_shapes=[pltpu.VMEM((PAIR, band_count, seq_count, time_len, HD), jnp.bfloat16)],
        compiler_params=params(),
        name="space_backward",
    )(q, k, v, probs, back)


def on_small_slice(q_space, k_space, v_space, q_time, k_time, out_weight, cotangent):
    seq_count, band_count = lax.axis_size("seq"), lax.axis_size("sub")
    time_len = q_space.shape[1] // band_count // seq_count
    me, sub, part = lax.axis_index("seq"), lax.axis_index("sub"), lax.axis_index("parts")
    ids = jnp.stack([me, sub, part]).astype(jnp.int32)
    rows, width = out_weight.shape

    half = lax.dynamic_slice_in_dim(out_weight, part * (rows // 2), rows // 2, 0)
    second = xor_send(half, "seq", 2)
    first = xor_send(half, "seq", 1)

    local = cotangent.shape[0]
    bounds = (0, width // 3, width)
    split = []
    for low, high in zip(bounds, bounds[1:]):
        picked = [cotangent[:, :, shard * width + low : shard * width + high] for shard in range(seq_count)]
        picked = jnp.concatenate(picked, axis=2)
        picked = picked.reshape(local, seq_count, time_len, -1).transpose(1, 0, 2, 3)
        split.append(picked.reshape(seq_count * local, time_len, -1))
    opening = split[0].reshape(seq_count, local, *split[0].shape[1:])
    opening = [lax.dynamic_index_in_dim(opening, me ^ step, 0, keepdims=False) for step in range(seq_count)]
    opening = [opening[0]] + [xor_send(opening[step], "seq", step) for step in range(1, seq_count)]
    q_space = after(q_space, split)
    mixed, probs = space_forward(q_space, k_space, v_space, seq_count, band_count, time_len)
    q_time = after(q_time, mixed)
    chances = time_probs(ids, q_time, k_time)
    first, second, opening, following, mixed = gate((first, second, opening, split[1], mixed), chances)
    here = [in_order(ids, opening), trade(following)]
    quarter = rows // 4
    third = [xor_send(second[:quarter], "seq", 1), None]
    other_near = swap_parts(jnp.concatenate([first, second], axis=0))
    across = [xor_send(here[0], "sub", 2), None]
    beside = [xor_send(here[0], "sub", 1), None]

    gated = gate((here[1], second, third[0], other_near, across[0], mixed), beside[0])
    here[1], second, third[0], other_near, across[0], mixed = gated
    moved = trade(mixed)
    third[1] = xor_send(second[quarter:], "seq", 1)
    third = jnp.concatenate(third, axis=0)
    across[1] = xor_send(here[1], "sub", 2)
    beside[1] = xor_send(here[1], "sub", 1)
    cross = [xor_send(across[0], "sub", 1), None]
    other_third = swap_parts(third)
    across[1] = after(across[1], (other_third, cross[0]))
    cross[1] = xor_send(across[1], "sub", 1)
    cots = []
    for side in range(2):
        cots += [here[side], beside[side], across[side], cross[side]]
    weights = [out_weight, first, second, third, other_near, other_third]

    turned, third_sum = weight_first(ids, chances, moved, cots)
    back = space_grad(ids, after(chances, third_sum), weights, cots, seq_count)
    returned = trade(back)
    second_sum, own_sum, first_sum = weight_second(ids, after(turned, back), cots, seq_count)
    third_sum = xor_send(third_sum, "seq", 1)
    paired = (second_sum + third_sum.astype(jnp.float32)).astype(jnp.bfloat16)
    far = xor_send(paired, "seq", 2)
    near = xor_send(after(first_sum, third_sum), "seq", 1)
    dq, dk, dv = space_backward(q_space, k_space, v_space, probs, returned)
    far, near = gate((far, near), dq)
    d_weight = own_sum + near.astype(jnp.float32) + far.astype(jnp.float32)
    return dq, dk, dv, d_weight


def solution(mesh):
    in_specs = (
        P(("parts", "seq"), None, "sub"),
        P(("parts", "seq"), None, "sub"),
        P(("parts", "seq"), None, "sub"),
        P("parts", None, "seq", "sub"),
        P("parts", None, "seq", "sub"),
        P("sub", "seq"),
        P(("parts", "seq"), "sub", None),
    )
    out_specs = (
        P(("parts", "seq"), None, "sub"),
        P(("parts", "seq"), None, "sub"),
        P(("parts", "seq"), None, "sub"),
        P(("parts", "sub"), "seq"),
    )
    small = (mesh.shape["parts"], mesh.shape["seq"], mesh.shape["sub"]) == (2, 4, 4)
    return jax.shard_map(
        on_small_slice if small else on_device, mesh=mesh, in_specs=in_specs, out_specs=out_specs, check_vma=False
    )
```
